128 devices in a mesh: dp: 4 (over z_lo, core), mp: 32 (over y, z_hi, x).
Axes of the slice: x: 4, y: 4, z: 4 (z_hi: 2, z_lo: 2; z = z_hi * 2 + z_lo), core: 2. Of those that a mesh axis runs over, the one named last changes fastest.
Arguments:
- fields: float32 [4, 32, 128, 128, 128], P('dp', None, 'mp'), may hold values from -6 to 6
- upstream: bfloat16 [4, 32, 128, 128, 128], P('dp', None, 'mp'), may hold values from -6 to 6
- spectral_weight: float32 [2, 32, 32, 32, 1024], P(None, None, None, 'dp', 'mp'), may hold values from -4.2 to 4.2
- point_weight: float32 [32, 32], replicated, may hold values from -1 to 1
- point_bias: float32 [32], replicated, may hold values from -3 to 3
Outputs:
- grad_fields: float32 [4, 32, 128, 128, 128], P('dp', None, 'mp')
- grad_weight: float32 [2, 32, 32, 32, 1024], P(None, None, None, 'dp', 'mp')
The draws below stay inside these ranges and needn't reach their ends.
All inputs are finite; a program needn't handle non-finite values.
Results may differ from the reference program's by a relative error of at most 0.0003.
Values sent between devices are 32-bit elements; how exact they have to be, the bound alone decides.
A program may use at most 256 MiB of HBM per device.

```python
import jax
import jax.numpy as jnp
from jax import lax

C = 32
NX = 128
NY = 128
NZ = 128
MX = 32
MY = 32
MZ = 32
BATCH = 4
MYZ = 1024


def block_levels(rng, extent, pieces, low, largest):
    loudness, own = 1.0, jax.random.fold_in(rng, 6)
    for axis_at, parts in pieces:
        draws = jnp.exp(jax.random.uniform(jax.random.fold_in(own, axis_at), (parts,), jnp.float32, low / len(pieces), largest / len(pieces)))
        loudness = loudness * jnp.repeat(draws, extent[axis_at] // parts).reshape([-1 if axis == axis_at else 1 for axis in range(len(extent))])
    return loudness


def normal_values(stream_key, dims, deviation, limit, split=(), held_as=jnp.bfloat16):
    factor_of = block_levels(stream_key, dims, split, -0.22, 0.18) if split else 1.0
    entries = jax.random.normal(stream_key, dims, jnp.float32) * deviation * factor_of
    return jnp.minimum(jnp.maximum(entries, -limit), limit).astype(held_as)


def setup_inputs(seed: int = 0) -> dict:
    splits = jax.random.split(jax.random.key(seed), 6)
    return {
        "fields": normal_values(splits[0], (BATCH, C, NX, NY, NZ), 1.0, 6.0, ((0, 4), (2, 32)), jnp.float32),
        "upstream": normal_values(splits[1], (BATCH, C, NX, NY, NZ), 1.0, 6.0, ((0, 4), (2, 32))),
        "spectral_weight": normal_values(splits[2], (2, C, C, MX, MYZ), 0.7, 4.2, ((3, 4), (4, 32)), jnp.float32),
        "point_weight": normal_values(splits[3], (C, C), C ** -0.5, 1.0, (), jnp.float32),
        "point_bias": normal_values(splits[4], (C,), 0.5, 3.0, (), jnp.float32),
    }


HIGHEST = lax.Precision.HIGHEST

def spectral(grid_field, weight):
    half_x = MX // 2
    half_y = MY // 2
    full_spec = jnp.fft.rfftn(grid_field, axes=(1, 2, 3))
    x_rows = jnp.concatenate([full_spec[:, :half_x], full_spec[:, NX - half_x:]], axis=1)
    kept_spec = jnp.concatenate([x_rows[:, :, :half_y], x_rows[:, :, NY - half_y:]], axis=2)[:, :, :, :MZ]
    coeffs = lax.complex(weight[0], weight[1]).reshape(C, C, MX, MY, MZ)
    mixed_spec = jnp.einsum('ixyz,ioxyz->oxyz', kept_spec, coeffs, precision=HIGHEST)
    padded = jnp.zeros((C, NX, NY, NZ // 2 + 1), mixed_spec.dtype)
    padded = padded.at[:, :half_x, :half_y, :MZ].set(mixed_spec[:, :half_x, :half_y])
    padded = padded.at[:, NX - half_x:, :half_y, :MZ].set(mixed_spec[:, half_x:, :half_y])
    padded = padded.at[:, :half_x, NY - half_y:, :MZ].set(mixed_spec[:, :half_x, half_y:])
    padded = padded.at[:, NX - half_x:, NY - half_y:, :MZ].set(mixed_spec[:, half_x:, half_y:])
    return jnp.fft.irfftn(padded, s=(NX, NY, NZ), axes=(1, 2, 3))

def reference(fields, upstream, spectral_weight, point_weight, point_bias):

    def layer_map(grid_field, weight):
        preact = spectral(grid_field, weight)
        preact = preact + jnp.einsum('cxyz,co->oxyz', grid_field, point_weight, precision=HIGHEST)
        preact = preact + point_bias[:, None, None, None]
        return jax.nn.gelu(preact, approximate=False)

    def sample_step(running, inputs_pair):
        grid_field, cotangent = inputs_pair
        activation, pullback = jax.vjp(layer_map, grid_field, spectral_weight)
        grad_field, grad_part = pullback(cotangent.astype(grid_field.dtype))
        return (running + grad_part, grad_field)
    running, grads = lax.scan(sample_step, jnp.zeros_like(spectral_weight), (fields, upstream))
    return (grads, running)
```

```python
from functools import partial

import jax
import jax.numpy as jnp
import ml_dtypes
import numpy as np
from jax import lax
from jax.experimental import pallas as pl
from jax.experimental.pallas import tpu as pltpu
from jax.sharding import PartitionSpec as P

N = 128
M = 32
C = 32
XL = 4
CG = 8
DP = 4
MP = 32
F32 = jnp.float32
BF16 = jnp.bfloat16
VMEM_LIMIT = 60 * 1024 * 1024


def split_np(table):
    table = table.astype(np.float32)
    high = table.astype(ml_dtypes.bfloat16)
    low = (table - high.astype(np.float32)).astype(ml_dtypes.bfloat16)
    return high, low


def angles(signed):
    frequency = np.arange(M)
    if signed:
        frequency = np.where(frequency < M // 2, frequency, frequency - M)
    phase = (np.arange(N)[:, None] * frequency[None, :]) % N
    theta = phase * (2.0 * np.pi / N)
    return np.cos(theta), np.sin(theta)


def make_tables():
    cz, sz = angles(False)
    cs, ss = angles(True)
    tz = np.zeros((4, N, 2, 4, M))
    for c in range(4):
        tz[c, :, 0, c, :] = cz
        tz[c, :, 1, c, :] = sz
    tz = tz.reshape(4 * N, 8 * M)
    ty = np.block([[cs.T, -ss.T], [-ss.T, -cs.T]])
    tx = np.zeros((2, M, N, 2))
    tx[0, :, :, 0] = cs.T
    tx[0, :, :, 1] = ss.T
    tx[1, :, :, 0] = -ss.T
    tx[1, :, :, 1] = cs.T
    tx = tx.reshape(2 * M, 2 * N)
    ix = np.zeros((N, 2, 2, M))
    ix[:, 0, 0] = cs
    ix[:, 0, 1] = -ss
    ix[:, 1, 0] = ss
    ix[:, 1, 1] = cs
    ix = ix.reshape(2 * N, 2 * M)
    iy = np.block([[cs, -ss], [ss, cs]])
    iz = np.zeros((2, 4, M, 4, N))
    for c in range(4):
        iz[0, c, :, c, :] = cz.T
        iz[1, c, :, c, :] = -sz.T
    iz = iz.reshape(8 * M, 4 * N)
    expand = np.repeat(np.eye(C), 8, axis=0)
    return {
        "tz": split_np(tz),
        "ty": split_np(ty),
        "tx": split_np(tx),
        "ix": split_np(ix),
        "iy": split_np(iy),
        "iz": split_np(iz),
        "expand": expand.astype(np.float32),
    }


TABLES = make_tables()


def split(value):
    high = value.astype(BF16)
    low = (value - high.astype(F32)).astype(BF16)
    return high, low


def mm(a, b):
    return jnp.dot(a, b, preferred_element_type=F32)


def left_table(table_h, table_l, data):
    high, low = split(data)
    return mm(table_h, high) + (mm(table_h, low) + mm(table_l, high))


def right_table(data, table_h, table_l):
    high, low = split(data)
    return mm(high, table_h) + (mm(low, table_h) + mm(high, table_l))


def params(limit=VMEM_LIMIT):
    return pltpu.CompilerParams(vmem_limit_bytes=limit)


def whole(shape):
    return pl.BlockSpec(shape, lambda *_: (0,) * len(shape))


def forward_tile(channels, tz_h, tz_l, ty_h, ty_l):
    rows = jnp.concatenate(channels, axis=1)
    along_z = right_table(rows, tz_h, tz_l)
    stacked = jnp.concatenate([along_z[:, :N], along_z[:, N:]], axis=0)
    return left_table(ty_h, ty_l, stacked)


def inverse_tile(modes, iy_h, iy_l, iz_h, iz_l):
    along_y = left_table(iy_h, iy_l, modes)
    merged = jnp.concatenate([along_y[:N], along_y[N:]], axis=1)
    return right_table(merged, iz_h, iz_l)


def factor_lanes():
    lane = lax.broadcasted_iota(jnp.int32, (8, N), 1)
    return jnp.where(lane % M == 0, 1.0, 2.0).astype(F32) * (1.0 / float(N * N * N))


def forward_plane_kernel(field_ref, tz_h, tz_l, ty_h, ty_l, out_ref):
    group = pl.program_id(0)
    tzh, tzl, tyh, tyl = tz_h[...], tz_l[...], ty_h[...], ty_l[...]
    for x in range(XL):
        tile = forward_tile([field_ref[c, x] for c in range(4)], tzh, tzl, tyh, tyl)
        for r in range(2):
            out_ref[pl.ds(group * 8 + 2 * x + r, M, stride=8 * CG), :] = tile[
                r * M : (r + 1) * M
            ]


def forward_plane(fields):
    tz, ty = TABLES["tz"], TABLES["ty"]
    return pl.pallas_call(
        forward_plane_kernel,
        grid=(CG,),
        in_specs=[
            pl.BlockSpec((4, XL, N, N), lambda g: (g, 0, 0, 0)),
            whole((4 * N, 8 * M)),
            whole((4 * N, 8 * M)),
            whole((2 * M, 2 * N)),
            whole((2 * M, 2 * N)),
        ],
        out_specs=whole((M * CG * 8, N)),
        out_shape=jax.ShapeDtypeStruct((M * CG * 8, N), F32),
        compiler_params=params(),
    )(fields, *map(jnp.asarray, tz + ty)).reshape(M, CG, 8, N)


def forward_x_kernel(in_ref, tx_h, tx_l, out_ref):
    txh, txl = tx_h[...], tx_l[...]
    for g in range(CG):
        tile = left_table(txh, txl, in_ref[:, g].reshape(2 * N, N))
        for r in range(2):
            for d in range(DP):
                out_ref[d, g, r] = tile[r * M + 8 * d : r * M + 8 * d + 8]


def forward_x(pieces):
    return pl.pallas_call(
        forward_x_kernel,
        out_shape=jax.ShapeDtypeStruct((DP, CG, 2, 8, N), F32),
        compiler_params=params(),
    )(pieces, *map(jnp.asarray, TABLES["tx"]))


def inverse_x_kernel(in_ref, ix_h, ix_l, out_ref):
    ixh, ixl = ix_h[...], ix_l[...]
    for g in range(CG):
        rows = jnp.concatenate(
            [in_ref[:, g, 0].reshape(M, N), in_ref[:, g, 1].reshape(M, N)], axis=0
        )
        out_ref[:, g] = left_table(ixh, ixl, rows).reshape(MP, 8, N)


def inverse_x(pieces):
    return pl.pallas_call(
        inverse_x_kernel,
        out_shape=jax.ShapeDtypeStruct((MP, CG, 8, N), F32),
        compiler_params=params(),
    )(pieces, *map(jnp.asarray, TABLES["ix"]))


def pack_kernel(w_ref, out_ref):
    @pl.loop(0, C)
    def _(o):
        for r in range(2):
            for g in range(w_ref.shape[1] // 4):
                out_ref[r, g, o] = jnp.concatenate(
                    [w_ref[r, 4 * g + q, o] for q in range(4)], axis=1
                )


def pack_weight(weight):
    return pl.pallas_call(
        pack_kernel,
        grid=(4,),
        in_specs=[pl.BlockSpec((2, 8, C, 8, M), lambda i: (0, i, 0, 0, 0))],
        out_specs=pl.BlockSpec((2, 2, C, 8, N), lambda i: (0, i, 0, 0, 0)),
        out_shape=jax.ShapeDtypeStruct((2, CG, C, 8, N), F32),
        compiler_params=params(),
    )(weight)


def lane_groups():
    return lax.broadcasted_iota(jnp.int32, (8, N), 1) // M


def pick(groups, tiles):
    low = jnp.where(groups == 0, tiles[0], tiles[1])
    high = jnp.where(groups == 2, tiles[2], tiles[3])
    return jnp.where(groups < 2, low, high)


def mix_kernel(spec_ref, w_ref, out_ref):
    groups = lane_groups()
    factor = factor_lanes()

    @pl.loop(0, CG)
    def _(g):
        totals = [[[] for _ in range(2)] for _ in range(DP)]
        for q in range(4):
            o = 4 * g + q
            acc = [[None, None] for _ in range(DP)]
            for i in range(CG):
                wr, wi = w_ref[0, i, o], w_ref[1, i, o]
                for b in range(DP):
                    sr, si = spec_ref[b, i, 0], spec_ref[b, i, 1]
                    re = wr * sr - wi * si
                    im = wr * si + wi * sr
                    acc[b] = [re, im] if i == 0 else [acc[b][0] + re, acc[b][1] + im]
            for b in range(DP):
                for r in range(2):
                    v = acc[b][r]
                    v = v + pltpu.roll(v, 64, 1)
                    totals[b][r].append(v + pltpu.roll(v, 32, 1))
        for b in range(DP):
            for r in range(2):
                out_ref[b, g, r] = pick(groups, totals[b][r]) * factor


def mix(spectrum, weight):
    return pl.pallas_call(
        mix_kernel,
        out_shape=jax.ShapeDtypeStruct((DP, CG, 2, 8, N), F32),
        compiler_params=params(),
    )(spectrum, weight)


def spread(grad_ref, rep_ref):
    groups = lane_groups()
    factor = factor_lanes()

    @pl.loop(0, CG)
    def _(g):
        for b in range(DP):
            for r in range(2):
                v = grad_ref[b, g, r] * factor
                rolled = [v] + [pltpu.roll(v, M * s, 1) for s in range(1, 4)]
                for q in range(4):
                    rep_ref[4 * g + q, b, r] = pick(
                        groups, [rolled[(h - q) % 4] for h in range(4)]
                    )


def back_mix_kernel(grad_ref, w_ref, out_ref, rep_ref):
    spread(grad_ref, rep_ref)

    @pl.loop(0, CG)
    def _(i):
        def step(t, acc):
            acc = list(acc)
            for u in range(4):
                o = 4 * t + u
                wr, wi = w_ref[0, i, o], w_ref[1, i, o]
                for b in range(DP):
                    gr, gi = rep_ref[o, b, 0], rep_ref[o, b, 1]
                    acc[2 * b] = acc[2 * b] + (wr * gr + wi * gi)
                    acc[2 * b + 1] = acc[2 * b + 1] + (wr * gi - wi * gr)
            return tuple(acc)

        acc = lax.fori_loop(0, 8, step, tuple(jnp.zeros((8, N), F32) for _ in range(8)))
        for b in range(DP):
            for r in range(2):
                out_ref[b, i, r] = acc[2 * b + r]


def back_mix(grad_spec, weight):
    return pl.pallas_call(
        back_mix_kernel,
        out_shape=jax.ShapeDtypeStruct((DP, CG, 2, 8, N), F32),
        scratch_shapes=[pltpu.VMEM((C, DP, 2, 8, N), F32)],
        compiler_params=params(),
    )(grad_spec, weight)


def weight_grad_kernel(grad_ref, spec_ref, out_ref, rep_ref):
    @pl.when(pl.program_id(0) == 0)
    def _():
        spread(grad_ref, rep_ref)

    @pl.loop(0, C)
    def _(o):
        for g in range(2):
            re = im = None
            for b in range(DP):
                gr, gi = rep_ref[o, b, 0], rep_ref[o, b, 1]
                sr, si = spec_ref[b, g, 0], spec_ref[b, g, 1]
                r1 = gr * sr + gi * si
                i1 = gi * sr - gr * si
                re, im = (r1, i1) if b == 0 else (re + r1, im + i1)
            for q in range(4):
                out_ref[0, 4 * g + q, o] = re[:, M * q : M * (q + 1)]
                out_ref[1, 4 * g + q, o] = im[:, M * q : M * (q + 1)]


def weight_grad(grad_spec, spectrum):
    return pl.pallas_call(
        weight_grad_kernel,
        grid=(4,),
        in_specs=[
            whole((DP, CG, 2, 8, N)),
            pl.BlockSpec((DP, 2, 2, 8, N), lambda i: (0, i, 0, 0, 0)),
        ],
        out_specs=pl.BlockSpec((2, 8, C, 8, M), lambda i: (0, i, 0, 0, 0)),
        out_shape=jax.ShapeDtypeStruct((2, C, C, 8, M), F32),
        scratch_shapes=[pltpu.VMEM((C, DP, 2, 8, N), F32)],
        compiler_params=params(),
    )(grad_spec, spectrum)


def channel_matrix(matrix, expand):
    spread_cols = lax.dot_general(
        matrix, expand, (((1,), (1,)), ((), ())), precision=lax.Precision.HIGHEST
    )
    full = jnp.dot(expand, spread_cols, precision=lax.Precision.HIGHEST)
    row = lax.broadcasted_iota(jnp.int32, (8 * C, 8 * C), 0)
    col = lax.broadcasted_iota(jnp.int32, (8 * C, 8 * C), 1)
    return split(jnp.where(row % 8 == col % 8, full, 0.0))


def spectral_plane(modes_ref, x, out_ref, tables):
    @pl.loop(0, CG)
    def _(g):
        modes = jnp.concatenate(
            [
                modes_ref[pl.ds(g * 8 + 2 * x + r, M, stride=8 * CG), :]
                for r in range(2)
            ],
            axis=0,
        )
        plane = inverse_tile(modes, *[t[...] for t in tables])
        for q in range(4):
            out_ref[4 * g + q] = plane[:, q * N : (q + 1) * N]


def channel_map(in_ref, y, mat_h, mat_l):
    data = jnp.concatenate(
        [in_ref[:, pl.ds(y + 8 * h, 8), :].reshape(8 * C, N) for h in range(2)], axis=1
    )
    return left_table(mat_h, mat_l, data)


def forward_cell_kernel(
    modes_ref, field_ref, up_ref, pw_ref, bias_ref, ex_ref,
    iy_h, iy_l, iz_h, iz_l, tz_h, tz_l, ty_h, ty_l,
    grad_ref, out_ref, mat_h, mat_l, pre_ref,
):
    x = pl.program_id(0)

    @pl.when(x == 0)
    def _():
        mat_h[...], mat_l[...] = channel_matrix(pw_ref[...].T, ex_ref[...])

    spectral_plane(modes_ref, x, pre_ref, (iy_h, iy_l, iz_h, iz_l))

    @pl.loop(0, N // 16)
    def _(t):
        y = pl.multiple_of(t * 16, 16)
        mapped = channel_map(field_ref, y, mat_h[...], mat_l[...])
        point = jnp.concatenate(
            [mapped[:, :N].reshape(C, 8, N), mapped[:, N:].reshape(C, 8, N)], axis=1
        )
        pre = pre_ref[:, pl.ds(y, 16), :] + point + bias_ref[...]
        cdf = 0.5 * (1.0 + lax.erf(pre * np.float32(np.sqrt(0.5))))
        slope = cdf + pre * (jnp.exp(-0.5 * pre * pre) * np.float32(1 / np.sqrt(2 * np.pi)))
        grad_ref[:, pl.ds(y, 16), :] = up_ref[:, pl.ds(y, 16), :].astype(F32) * slope

    @pl.loop(0, CG)
    def _(g):
        tile = forward_tile(
            [grad_ref[4 * g + q] for q in range(4)], tz_h[...], tz_l[...], ty_h[...], ty_l[...]
        )
        for r in range(2):
            out_ref[pl.ds(g * 8 + 2 * x + r, M, stride=8 * CG), :] = tile[r * M : (r + 1) * M]


def plane_spec():
    return pl.BlockSpec((C, pl.Squeezed(), N, N), lambda x: (0, x, 0, 0))


def forward_cells(modes, fields, upstream, point_weight, point_bias):
    tabs = TABLES["iy"] + TABLES["iz"] + TABLES["tz"] + TABLES["ty"]
    grad_pre, out = pl.pallas_call(
        forward_cell_kernel,
        grid=(XL,),
        in_specs=[
            whole((M * CG * 8, N)),
            plane_spec(),
            plane_spec(),
            whole((C, C)),
            whole((C, 1, N)),
            whole((8 * C, C)),
        ]
        + [whole(t.shape) for t in tabs],
        out_specs=[plane_spec(), whole((M * CG * 8, N))],
        out_shape=[
            jax.ShapeDtypeStruct((C, XL, N, N), F32),
            jax.ShapeDtypeStruct((M * CG * 8, N), F32),
        ],
        scratch_shapes=[
            pltpu.VMEM((8 * C, 8 * C), BF16),
            pltpu.VMEM((8 * C, 8 * C), BF16),
            pltpu.VMEM((C, N, N), F32),
        ],
        compiler_params=params(),
    )(
        modes.reshape(M * CG * 8, N),
        fields,
        upstream,
        point_weight,
        jnp.broadcast_to(point_bias[:, None, None], (C, 1, N)),
        jnp.asarray(TABLES["expand"]),
        *map(jnp.asarray, tabs),
    )
    return grad_pre, out.reshape(M, CG, 8, N)


def backward_cell_kernel(
    modes_ref, grad_ref, pw_ref, ex_ref, iy_h, iy_l, iz_h, iz_l, out_ref, mat_h, mat_l
):
    x = pl.program_id(0)

    @pl.when(x == 0)
    def _():
        mat_h[...], mat_l[...] = channel_matrix(pw_ref[...], ex_ref[...])

    spectral_plane(modes_ref, x, out_ref, (iy_h, iy_l, iz_h, iz_l))

    @pl.loop(0, N // 16)
    def _(t):
        y = pl.multiple_of(t * 16, 16)
        mapped = channel_map(grad_ref, y, mat_h[...], mat_l[...])
        for h in range(2):
            at = pl.ds(y + 8 * h, 8)
            out_ref[:, at, :] = out_ref[:, at, :] + mapped[:, h * N : (h + 1) * N].reshape(C, 8, N)


def backward_cells(modes, grad_pre, point_weight):
    tabs = TABLES["iy"] + TABLES["iz"]
    return pl.pallas_call(
        backward_cell_kernel,
        grid=(XL,),
        in_specs=[whole((M * CG * 8, N)), plane_spec(), whole((C, C)), whole((8 * C, C))]
        + [whole(t.shape) for t in tabs],
        out_specs=plane_spec(),
        out_shape=jax.ShapeDtypeStruct((C, XL, N, N), F32),
        scratch_shapes=[pltpu.VMEM((8 * C, 8 * C), BF16), pltpu.VMEM((8 * C, 8 * C), BF16)],
        compiler_params=params(),
    )(
        modes.reshape(M * CG * 8, N),
        grad_pre,
        point_weight,
        jnp.asarray(TABLES["expand"]),
        *map(jnp.asarray, tabs),
    )


def swap(pieces, axis):
    return lax.all_to_all(pieces, axis, split_axis=0, concat_axis=0, tiled=True)


def shards(fields, upstream, spectral_weight, point_weight, point_bias):
    fields = fields[0]
    upstream = upstream[0]
    weight = pack_weight(spectral_weight)
    spectrum = swap(forward_x(swap(forward_plane(fields), "mp")), "dp")
    mixed = mix(spectrum, weight)
    modes = swap(inverse_x(swap(mixed, "dp")), "mp")
    grad_pre, pieces = forward_cells(modes, fields, upstream, point_weight, point_bias)
    grad_spec = swap(forward_x(swap(pieces, "mp")), "dp")
    back = back_mix(grad_spec, weight)
    weight_out = weight_grad(grad_spec, spectrum)
    modes = swap(inverse_x(swap(back, "dp")), "mp")
    grad_fields = backward_cells(modes, grad_pre, point_weight)
    return (grad_fields[None], weight_out)


def solution(mesh):
    placed = (
        P("dp", None, "mp", None, None),
        P("dp", None, "mp", None, None),
        P(None, None, None, "dp", "mp"),
        P(),
        P(),
    )
    return jax.shard_map(
        shards,
        mesh=mesh,
        in_specs=placed,
        out_specs=(P("dp", None, "mp", None, None), P(None, None, None, "dp", "mp")),
        check_vma=False,
    )
```

```python
from functools import partial

import jax
import jax.numpy as jnp
import ml_dtypes
import numpy as np
from jax import lax
from jax.experimental import pallas as pl
from jax.experimental.pallas import tpu as pltpu
from jax.sharding import PartitionSpec as P

N = 128
M = 32
C = 32
XL = 4
CG = 8
DP = 4
MP = 32
F32 = jnp.float32
BF16 = jnp.bfloat16
VMEM_LIMIT = 60 * 1024 * 1024


def split_np(table):
    table = table.astype(np.float32)
    high = table.astype(ml_dtypes.bfloat16)
    low = (table - high.astype(np.float32)).astype(ml_dtypes.bfloat16)
    return high, low


def angles(signed):
    frequency = np.arange(M)
    if signed:
        frequency = np.where(frequency < M // 2, frequency, frequency - M)
    phase = (np.arange(N)[:, None] * frequency[None, :]) % N
    theta = phase * (2.0 * np.pi / N)
    return np.cos(theta), np.sin(theta)


def make_tables():
    cz, sz = angles(False)
    cs, ss = angles(True)
    tz = np.zeros((4, N, 2, 4, M))
    for c in range(4):
        tz[c, :, 0, c, :] = cz
        tz[c, :, 1, c, :] = sz
    tz = tz.reshape(4 * N, 8 * M)
    ty = np.block([[cs.T, -ss.T], [-ss.T, -cs.T]])
    tx = np.zeros((2, M, N, 2))
    tx[0, :, :, 0] = cs.T
    tx[0, :, :, 1] = ss.T
    tx[1, :, :, 0] = -ss.T
    tx[1, :, :, 1] = cs.T
    tx = tx.reshape(2 * M, 2 * N)
    ix = np.zeros((N, 2, 2, M))
    ix[:, 0, 0] = cs
    ix[:, 0, 1] = -ss
    ix[:, 1, 0] = ss
    ix[:, 1, 1] = cs
    ix = ix.reshape(2 * N, 2 * M)
    iy = np.block([[cs, -ss], [ss, cs]])
    iz = np.zeros((2, 4, M, 4, N))
    for c in range(4):
        iz[0, c, :, c, :] = cz.T
        iz[1, c, :, c, :] = -sz.T
    iz = iz.reshape(8 * M, 4 * N)
    expand = np.repeat(np.eye(C), 8, axis=0)
    return {
        "tz": split_np(tz),
        "ty": split_np(ty),
        "tx": split_np(tx),
        "ix": split_np(ix),
        "iy": split_np(iy),
        "iz": split_np(iz),
        "expand": expand.astype(np.float32),
    }


TABLES = make_tables()


def thrice(pair, axis):
    high, low = pair
    return np.concatenate([high, high, low], axis=axis)


TZ = thrice(TABLES["tz"], 0)
TY = np.concatenate(TABLES["ty"], axis=0)
TX = np.concatenate(TABLES["tx"], axis=0)
IX = thrice(TABLES["ix"], 1)
IY = thrice(TABLES["iy"], 1)
IZ = thrice(TABLES["iz"], 0)
EXPAND = TABLES["expand"]


def split(value):
    high = value.astype(BF16)
    low = (value - high.astype(F32)).astype(BF16)
    return high, low


def mm(a, b):
    return jnp.dot(a, b, preferred_element_type=F32)


def whole(shape):
    return pl.BlockSpec(shape, lambda *_: (0,) * len(shape))


NQ = 4
GQ = CG // NQ
RQ = 8 * GQ
MESH = pl.DeviceIdType.MESH


def position():
    return lax.axis_index("dp"), lax.axis_index("mp")


def greet():
    dp, mp = position()
    barrier = pltpu.get_barrier_semaphore()

    @pl.loop(1, MP)
    def _(k):
        pl.semaphore_signal(
            barrier, inc=1, device_id=(dp, lax.rem(mp + k, MP)), device_id_type=MESH
        )

    for k in range(1, DP):
        pl.semaphore_signal(
            barrier, inc=1, device_id=(lax.rem(dp + k, DP), mp), device_id_type=MESH
        )


def await_greetings():
    pl.semaphore_wait(pltpu.get_barrier_semaphore(), MP - 1 + DP - 1)


def flat_rows(device, q):
    return pl.ds(pl.multiple_of(device * 64 + q * RQ, 8), RQ)


def piece_rows(q):
    return pl.ds(pl.multiple_of(q * RQ, 8), RQ)


def send_to_modes(q, flat, pieces, send_sem, recv_sem):
    dp, mp = position()

    @pl.loop(1, MP)
    def _(k):
        peer = lax.rem(mp + k, MP)
        pltpu.make_async_remote_copy(
            src_ref=flat.at[flat_rows(peer, q)],
            dst_ref=pieces.at[mp, piece_rows(q)],
            send_sem=send_sem.at[q],
            recv_sem=recv_sem.at[q],
            device_id=(dp, peer),
            device_id_type=MESH,
        ).start()


def send_to_cells(q, pieces, flat, send_sem, recv_sem):
    dp, mp = position()

    @pl.loop(1, MP)
    def _(k):
        peer = lax.rem(mp + k, MP)
        pltpu.make_async_remote_copy(
            src_ref=pieces.at[peer, piece_rows(q)],
            dst_ref=flat.at[flat_rows(mp, q)],
            send_sem=send_sem.at[q],
            recv_sem=recv_sem.at[q],
            device_id=(dp, peer),
            device_id_type=MESH,
        ).start()


def drain_mp(q, flat, sem):
    part = flat.at[pl.ds(0, (MP - 1) * RQ)]
    pltpu.make_async_copy(part, part, sem.at[q]).wait()


def send_dp(q, src, dst, send_sem, recv_sem):
    dp, mp = position()
    groups = pl.ds(q * GQ, GQ)
    for k in range(1, DP):
        peer = lax.rem(dp + k, DP)
        pltpu.make_async_remote_copy(
            src_ref=src.at[peer, groups],
            dst_ref=dst.at[dp, groups],
            send_sem=send_sem.at[q],
            recv_sem=recv_sem.at[q],
            device_id=(peer, mp),
            device_id_type=MESH,
        ).start()


def keep_dp(q, src, dst):
    dp, _ = position()
    groups = pl.ds(q * GQ, GQ)
    dst[dp, groups] = src[dp, groups]


def drain_dp(q, ref, sem):
    part = ref.at[pl.ds(0, DP - 1), pl.ds(0, GQ)]
    pltpu.make_async_copy(part, part, sem.at[q]).wait()


def chunks(body):
    @pl.loop(0, NQ)
    def _(q):
        body(q)


def groups_of(q, body):
    @pl.loop(0, GQ)
    def _(h):
        body(q * GQ + h)


def forward_group(field_ref, g, tz, ty, flat):
    rows = jnp.concatenate([field_ref[4 * g + c].reshape(XL * N, N) for c in range(4)], axis=1)
    high, low = split(rows)
    along_z = mm(jnp.concatenate([high, low, high], axis=1), tz[...])
    stacked = jnp.concatenate(
        [
            jnp.concatenate(
                [along_z[x * N : (x + 1) * N, :N], along_z[x * N : (x + 1) * N, N:]], axis=0
            )
            for x in range(XL)
        ],
        axis=1,
    )
    high, low = split(stacked)
    tables = ty[...]
    both = mm(tables, high)
    tile = both[: 2 * M] + both[2 * M :] + mm(tables[: 2 * M], low)
    for x in range(XL):
        for r in range(2):
            flat[pl.ds(g * 8 + 2 * x + r, M, stride=64), :] = tile[
                r * M : (r + 1) * M, x * N : (x + 1) * N
            ]


def inverse_group(flat, g, iy, iz):
    modes = jnp.concatenate(
        [
            jnp.concatenate(
                [flat[pl.ds(g * 8 + 2 * x + r, M, stride=64), :] for r in range(2)], axis=0
            )
            for x in range(XL)
        ],
        axis=1,
    )
    high, low = split(modes)
    along_y = mm(iy[...], jnp.concatenate([high, low, high], axis=0))
    rows = jnp.concatenate(
        [
            jnp.concatenate(
                [along_y[:N, x * N : (x + 1) * N], along_y[N:, x * N : (x + 1) * N]], axis=1
            )
            for x in range(XL)
        ],
        axis=0,
    )
    high, low = split(rows)
    return mm(jnp.concatenate([high, low, high], axis=1), iz[...])


def forward_x(pieces, g, tx, out):
    data = pieces[:, pl.ds(pl.multiple_of(g * 8, 8), 8), :].reshape(2 * N, N)
    high, low = split(data)
    tables = tx[...]
    both = mm(tables, high)
    tile = both[: 2 * M] + both[2 * M :] + mm(tables[: 2 * M], low)
    for d in range(DP):
        for r in range(2):
            out[d, g, r] = tile[r * M + 8 * d : r * M + 8 * d + 8]


def inverse_x(modes, g, ix, pieces):
    rows = jnp.concatenate([modes[:, g, 0].reshape(M, N), modes[:, g, 1].reshape(M, N)], axis=0)
    high, low = split(rows)
    tile = mm(ix[...], jnp.concatenate([high, low, high], axis=0))
    pieces[:, pl.ds(pl.multiple_of(g * 8, 8), 8), :] = tile.reshape(MP, 8, N)


def channel_matrix(matrix, expand, mat):
    spread_cols = lax.dot_general(
        matrix, expand, (((1,), (1,)), ((), ())), precision=lax.Precision.HIGHEST
    )
    full = jnp.dot(expand, spread_cols, precision=lax.Precision.HIGHEST)
    row = lax.broadcasted_iota(jnp.int32, (8 * C, 8 * C), 0)
    col = lax.broadcasted_iota(jnp.int32, (8 * C, 8 * C), 1)
    high, low = split(jnp.where(row % 8 == col % 8, full, 0.0))
    mat[: 8 * C] = high
    mat[8 * C :] = low


YB = 4


def channel_map(in_ref, x, mat, out_ref):
    @pl.loop(0, N // (8 * YB))
    def _(t):
        y = pl.multiple_of(t * 8 * YB, 8)
        data = jnp.concatenate(
            [in_ref[:, x, pl.ds(y + 8 * h, 8), :].reshape(8 * C, N) for h in range(YB)], axis=1
        )
        high, low = split(data)
        tables = mat[...]
        both = mm(tables, high)
        mapped = both[: 8 * C] + both[8 * C :] + mm(tables[: 8 * C], low)
        for h in range(YB):
            out_ref[:, x, pl.ds(y + 8 * h, 8), :] = mapped[:, h * N : (h + 1) * N].reshape(C, 8, N)


def factor_lanes():
    lane = lax.broadcasted_iota(jnp.int32, (8, N), 1)
    return jnp.where(lane % M == 0, 1.0, 2.0).astype(F32) * (1.0 / float(N * N * N))


def lane_groups():
    return lax.broadcasted_iota(jnp.int32, (8, N), 1) // M


def pick(groups, tiles):
    low = jnp.where(groups == 0, tiles[0], tiles[1])
    high = jnp.where(groups == 2, tiles[2], tiles[3])
    return jnp.where(groups < 2, low, high)


def mix(spec_ref, w_ref, g, out_ref):
    groups = lane_groups()
    factor = factor_lanes()
    totals = [[[] for _ in range(2)] for _ in range(DP)]
    for q in range(4):
        o = 4 * g + q
        acc = [[None, None] for _ in range(DP)]
        for i in range(CG):
            wr, wi = w_ref[0, i, o], w_ref[1, i, o]
            for b in range(DP):
                sr, si = spec_ref[b, i, 0], spec_ref[b, i, 1]
                re = wr * sr - wi * si
                im = wr * si + wi * sr
                acc[b] = [re, im] if i == 0 else [acc[b][0] + re, acc[b][1] + im]
        for b in range(DP):
            for r in range(2):
                v = acc[b][r]
                v = v + pltpu.roll(v, 64, 1)
                totals[b][r].append(v + pltpu.roll(v, 32, 1))
    for b in range(DP):
        for r in range(2):
            out_ref[b, g, r] = pick(groups, totals[b][r]) * factor


def spread(grad_ref, rep_ref):
    groups = lane_groups()
    factor = factor_lanes()

    @pl.loop(0, CG)
    def _(g):
        for b in range(DP):
            for r in range(2):
                v = grad_ref[b, g, r] * factor
                rolled = [v] + [pltpu.roll(v, M * s, 1) for s in range(1, 4)]
                for q in range(4):
                    rep_ref[4 * g + q, b, r] = pick(
                        groups, [rolled[(h - q) % 4] for h in range(4)]
                    )


def back_mix(rep_ref, w_ref, i, out_ref):
    def step(t, acc):
        acc = list(acc)
        for u in range(4):
            o = 4 * t + u
            wr, wi = w_ref[0, i, o], w_ref[1, i, o]
            for b in range(DP):
                gr, gi = rep_ref[o, b, 0], rep_ref[o, b, 1]
                acc[2 * b] = acc[2 * b] + (wr * gr + wi * gi)
                acc[2 * b + 1] = acc[2 * b + 1] + (wr * gi - wi * gr)
        return tuple(acc)

    acc = lax.fori_loop(0, 8, step, tuple(jnp.zeros((8, N), F32) for _ in range(8)))
    for b in range(DP):
        for r in range(2):
            out_ref[b, i, r] = acc[2 * b + r]


def weight_grad(rep_ref, spec_ref, o, out_ref):
    grads = [[rep_ref[o, b, r] for r in range(2)] for b in range(DP)]
    for i in range(CG):
        re = im = None
        for b in range(DP):
            gr, gi = grads[b]
            sr, si = spec_ref[b, i, 0], spec_ref[b, i, 1]
            r1 = gr * sr + gi * si
            i1 = gi * sr - gr * si
            re, im = (r1, i1) if b == 0 else (re + r1, im + i1)
        out_ref[0, i, o] = re
        out_ref[1, i, o] = im


def params(collective_id=None):
    if collective_id is None:
        return pltpu.CompilerParams(vmem_limit_bytes=VMEM_LIMIT)
    return pltpu.CompilerParams(
        vmem_limit_bytes=VMEM_LIMIT, collective_id=collective_id, has_side_effects=True
    )


def in_vmem():
    return pl.BlockSpec(memory_space=pltpu.VMEM)


def anywhere():
    return pl.BlockSpec(memory_space=pl.ANY)


def sems(count):
    return pltpu.SemaphoreType.DMA((count,))


SPEC = (DP, CG, 2, 8, N)
FLAT = (M * 64, N)
PIECES = (MP, 64, N)
CELLS = (C, XL, N, N)
PACKED = (2, CG, C, 8, N)


def to_spectrum(flat, pieces, held, out, tx, mp_sems, dp_sems):
    _, mp = position()

    def body(q):
        drain_mp(q, flat, mp_sems[1])
        pieces[mp, piece_rows(q)] = flat[flat_rows(mp, q)]
        groups_of(q, lambda g: forward_x(pieces, g, tx, held))
        send_dp(q, held, out, *dp_sems)
        keep_dp(q, held, out)

    chunks(body)


def start_kernel(
    field_ref, w_ref, tz, ty, tx, spec_ref, packed_ref,
    fields, weight, flat, pieces, held, landed,
    field_sem, weight_sem, mp_send, mp_recv, dp_send, dp_recv,
):
    greet()

    def field_copy(g):
        part = pl.ds(4 * g, 4)
        return pltpu.make_async_copy(field_ref.at[part], fields.at[part], field_sem.at[g])

    @pl.loop(0, CG)
    def _(g):
        field_copy(g).start()

    weight_copy = pltpu.make_async_copy(w_ref, weight, weight_sem.at[0])
    weight_copy.start()

    def transform(g):
        field_copy(g).wait()
        forward_group(fields, g, tz, ty, flat)

    def body(q):
        groups_of(q, transform)

        @pl.when(q == 0)
        def _():
            await_greetings()

        send_to_modes(q, flat, pieces, mp_send, mp_recv)

    chunks(body)
    weight_copy.wait()

    @pl.loop(0, C)
    def _(o):
        for r in range(2):
            for g in range(CG):
                packed_ref[r, g, o] = jnp.concatenate(
                    [weight[r, 4 * g + q, o] for q in range(4)], axis=1
                )

    to_spectrum(flat, pieces, held, landed, tx, (mp_send, mp_recv), (dp_send, dp_recv))
    chunks(lambda q: drain_dp(q, landed, dp_recv))
    spec_ref[...] = landed[...]
    chunks(lambda q: drain_mp(q, flat, mp_send))
    chunks(lambda q: drain_dp(q, landed, dp_send))


def start(fields, weight):
    tabs = [TZ, TY, TX]
    return pl.pallas_call(
        start_kernel,
        in_specs=[anywhere(), anywhere()] + [in_vmem()] * len(tabs),
        out_specs=[in_vmem(), in_vmem()],
        out_shape=[jax.ShapeDtypeStruct(SPEC, F32), jax.ShapeDtypeStruct(PACKED, F32)],
        scratch_shapes=[
            pltpu.VMEM(CELLS, F32),
            pltpu.VMEM((2, C, C, 8, M), F32),
            pltpu.VMEM(FLAT, F32),
            pltpu.VMEM(PIECES, F32),
            pltpu.VMEM(SPEC, F32),
            pltpu.VMEM(SPEC, F32),
            sems(CG),
            sems(1),
        ]
        + [sems(NQ)] * 4,
        compiler_params=params(1),
    )(fields, weight, *map(jnp.asarray, tabs))


def plane_copy(src, dst, sem, x):
    return pltpu.make_async_copy(src.at[:, x], dst.at[:, x], sem.at[x])


def to_planes(modes, pieces, flat, ix, mp_sems, dp_recv):
    def body(q):
        drain_dp(q, modes, dp_recv)
        groups_of(q, lambda g: inverse_x(modes, g, ix, pieces))
        send_to_cells(q, pieces, flat, *mp_sems)

    chunks(body)


def middle_kernel(
    spec_ref, packed_ref, field_ref, up_ref, pw_ref, bias_ref, ex_ref, ix, iy, iz, tz, ty, tx,
    spec_out, grad_out,
    fields, upstream, cells, mat, mixed, modes, ipieces, iflat, flat, pieces, held, landed,
    field_sem, up_sem, grad_sem,
    d1_send, d1_recv, m1_send, m1_recv, m2_send, m2_recv, d2_send, d2_recv,
):
    _, mp = position()
    greet()
    for x in range(XL):
        plane_copy(field_ref, fields, field_sem, x).start()
    up_copy = pltpu.make_async_copy(up_ref, upstream, up_sem.at[0])
    up_copy.start()

    def mix_chunk(q):
        groups_of(q, lambda g: mix(spec_ref, packed_ref, g, mixed))

        @pl.when(q == 0)
        def _():
            await_greetings()

        send_dp(q, mixed, modes, d1_send, d1_recv)
        keep_dp(q, mixed, modes)

    chunks(mix_chunk)
    channel_matrix(pw_ref[...].T, ex_ref[...], mat)

    def point(x):
        plane_copy(field_ref, fields, field_sem, x).wait()
        channel_map(fields, x, mat, cells)

    to_planes(modes, ipieces, iflat, ix, (m1_send, m1_recv), d1_recv)

    @pl.loop(0, XL)
    def _(x):
        point(x)

    up_copy.wait()

    def cell_group(g):
        spectral = inverse_group(iflat, g, iy, iz)
        for c in range(4):
            cells[4 * g + c] = (
                cells[4 * g + c]
                + spectral[:, c * N : (c + 1) * N].reshape(XL, N, N)
                + bias_ref[4 * g + c]
            )

        @pl.loop(0, 4 * XL)
        def _(t):
            o, x = 4 * g + t // XL, t % XL
            pre = cells[o, x]
            cdf = 0.5 * (1.0 + lax.erf(pre * np.float32(np.sqrt(0.5))))
            density = jnp.exp(-0.5 * pre * pre) * np.float32(1 / np.sqrt(2 * np.pi))
            cells[o, x] = upstream[o, x].astype(F32) * (cdf + pre * density)

        forward_group(cells, g, tz, ty, flat)

    def grad_copy(q):
        part = pl.ds(q * 4 * GQ, 4 * GQ)
        return pltpu.make_async_copy(cells.at[part], grad_out.at[part], grad_sem.at[q])

    def cell_chunk(q):
        drain_mp(q, iflat, m1_recv)
        iflat[flat_rows(mp, q)] = ipieces[mp, piece_rows(q)]
        groups_of(q, cell_group)
        send_to_modes(q, flat, pieces, m2_send, m2_recv)
        grad_copy(q).start()

    chunks(cell_chunk)
    to_spectrum(flat, pieces, held, landed, tx, (m2_send, m2_recv), (d2_send, d2_recv))
    chunks(lambda q: drain_dp(q, landed, d2_recv))
    spec_out[...] = landed[...]
    chunks(lambda q: drain_dp(q, landed, d1_send))
    chunks(lambda q: drain_dp(q, landed, d2_send))
    chunks(lambda q: drain_mp(q, flat, m1_send))
    chunks(lambda q: drain_mp(q, flat, m2_send))
    chunks(lambda q: grad_copy(q).wait())


def middle(spectrum, packed, fields, upstream, point_weight, point_bias):
    tabs = [IX, IY, IZ, TZ, TY, TX]
    return pl.pallas_call(
        middle_kernel,
        in_specs=[in_vmem(), in_vmem(), anywhere(), anywhere()] + [in_vmem()] * (3 + len(tabs)),
        out_specs=[in_vmem(), anywhere()],
        out_shape=[jax.ShapeDtypeStruct(SPEC, F32), jax.ShapeDtypeStruct(CELLS, F32)],
        scratch_shapes=[
            pltpu.VMEM(CELLS, F32),
            pltpu.VMEM(CELLS, BF16),
            pltpu.VMEM(CELLS, F32),
            pltpu.VMEM((16 * C, 8 * C), BF16),
            pltpu.VMEM(SPEC, F32),
            pltpu.VMEM(SPEC, F32),
            pltpu.VMEM(PIECES, F32),
            pltpu.VMEM(FLAT, F32),
            pltpu.VMEM(FLAT, F32),
            pltpu.VMEM(PIECES, F32),
            pltpu.VMEM(SPEC, F32),
            pltpu.VMEM(SPEC, F32),
            sems(XL),
            sems(1),
            sems(NQ),
        ]
        + [sems(NQ)] * 8,
        compiler_params=params(2),
    )(
        spectrum,
        packed,
        fields,
        upstream,
        point_weight,
        jnp.broadcast_to(point_bias[:, None, None], (C, 1, N)),
        jnp.asarray(EXPAND),
        *map(jnp.asarray, tabs),
    )


def back_kernel(
    grad_spec, spec_ref, packed_ref, grad_ref, pw_ref, ex_ref, ix,
    flat_out, wgrad_out, point_out,
    rep, grads, point, mat, mixed, modes, pieces, flat,
    grad_sem, point_sem, d_send, d_recv, m_send, m_recv,
):
    _, mp = position()
    greet()
    for x in range(XL):
        plane_copy(grad_ref, grads, grad_sem, x).start()
    spread(grad_spec, rep)

    def mix_chunk(q):
        groups_of(q, lambda i: back_mix(rep, packed_ref, i, mixed))

        @pl.when(q == 0)
        def _():
            await_greetings()

        send_dp(q, mixed, modes, d_send, d_recv)
        keep_dp(q, mixed, modes)

    chunks(mix_chunk)
    channel_matrix(pw_ref[...], ex_ref[...], mat)
    to_planes(modes, pieces, flat, ix, (m_send, m_recv), d_recv)

    @pl.loop(0, C)
    def _(o):
        weight_grad(rep, spec_ref, o, wgrad_out)

    @pl.loop(0, XL)
    def _(x):
        plane_copy(grad_ref, grads, grad_sem, x).wait()
        channel_map(grads, x, mat, point)
        plane_copy(point, point_out, point_sem, x).start()

    def land(q):
        drain_mp(q, flat, m_recv)
        flat[flat_rows(mp, q)] = pieces[mp, piece_rows(q)]

    chunks(land)
    flat_out[...] = flat[...]
    chunks(lambda q: drain_dp(q, modes, d_send))
    chunks(lambda q: drain_mp(q, flat, m_send))
    for x in range(XL):
        plane_copy(point, point_out, point_sem, x).wait()


def back(grad_spec, spectrum, packed, grad_pre, point_weight):
    return pl.pallas_call(
        back_kernel,
        in_specs=[in_vmem(), in_vmem(), in_vmem(), anywhere(), in_vmem(), in_vmem(), in_vmem()],
        out_specs=[in_vmem(), in_vmem(), anywhere()],
        out_shape=[
            jax.ShapeDtypeStruct(FLAT, F32),
            jax.ShapeDtypeStruct(PACKED, F32),
            jax.ShapeDtypeStruct(CELLS, F32),
        ],
        scratch_shapes=[
            pltpu.VMEM((C, DP, 2, 8, N), F32),
            pltpu.VMEM(CELLS, F32),
            pltpu.VMEM(CELLS, F32),
            pltpu.VMEM((16 * C, 8 * C), BF16),
            pltpu.VMEM(SPEC, F32),
            pltpu.VMEM(SPEC, F32),
            pltpu.VMEM(PIECES, F32),
            pltpu.VMEM(FLAT, F32),
            sems(XL),
            sems(XL),
        ]
        + [sems(NQ)] * 4,
        compiler_params=params(3),
    )(grad_spec, spectrum, packed, grad_pre, point_weight, jnp.asarray(EXPAND), jnp.asarray(IX))


def finish_kernel(flat, point, wgrad, iy, iz, cells_out, wgrad_out):
    g = pl.program_id(0)
    spectral = inverse_group(flat, g, iy, iz)
    for c in range(4):
        cells_out[c] = point[c] + spectral[:, c * N : (c + 1) * N].reshape(XL, N, N)

    @pl.loop(0, C // 4)
    def _(t):
        for u in range(4):
            for r in range(2):
                tile = wgrad[r, t * 4 + u]
                for q in range(4):
                    wgrad_out[r, q, t * 4 + u] = tile[:, M * q : M * (q + 1)]


def finish(flat, point, wgrad):
    cell_spec = pl.BlockSpec((4, XL, N, N), lambda g: (g, 0, 0, 0))
    return pl.pallas_call(
        finish_kernel,
        grid=(CG,),
        in_specs=[
            whole(FLAT),
            cell_spec,
            pl.BlockSpec((2, pl.Squeezed(), C, 8, N), lambda g: (0, g, 0, 0, 0)),
            whole(IY.shape),
            whole(IZ.shape),
        ],
        out_specs=[cell_spec, pl.BlockSpec((2, 4, C, 8, M), lambda g: (0, g, 0, 0, 0))],
        out_shape=[
            jax.ShapeDtypeStruct(CELLS, F32),
            jax.ShapeDtypeStruct((2, C, C, 8, M), F32),
        ],
        compiler_params=params(),
    )(flat, point, wgrad, jnp.asarray(IY), jnp.asarray(IZ))


def shards(fields, upstream, spectral_weight, point_weight, point_bias):
    fields = fields[0]
    spectrum, packed = start(fields, spectral_weight)
    grad_spec, grad_pre = middle(
        spectrum, packed, fields, upstream[0], point_weight, point_bias
    )
    flat, wgrad, point = back(grad_spec, spectrum, packed, grad_pre, point_weight)
    grad_fields, weight_out = finish(flat, point, wgrad)
    return (grad_fields[None], weight_out)


def solution(mesh):
    placed = (
        P("dp", None, "mp", None, None),
        P("dp", None, "mp", None, None),
        P(None, None, None, "dp", "mp"),
        P(),
        P(),
    )
    return jax.shard_map(
        shards,
        mesh=mesh,
        in_specs=placed,
        out_specs=(P("dp", None, "mp", None, None), P(None, None, None, "dp", "mp")),
        check_vma=False,
    )
```

```python
from functools import partial

import jax
import jax.numpy as jnp
import ml_dtypes
import numpy as np
from jax import lax
from jax.experimental import pallas as pl
from jax.experimental.pallas import tpu as pltpu
from jax.sharding import PartitionSpec as P

N = 128
M = 32
C = 32
XL = 4
CG = 8
DP = 4
MP = 32
F32 = jnp.float32
BF16 = jnp.bfloat16
VMEM_LIMIT = 60 * 1024 * 1024


def split_np(table):
    table = table.astype(np.float32)
    high = table.astype(ml_dtypes.bfloat16)
    low = (table - high.astype(np.float32)).astype(ml_dtypes.bfloat16)
    return high, low


def angles(signed):
    frequency = np.arange(M)
    if signed:
        frequency = np.where(frequency < M // 2, frequency, frequency - M)
    phase = (np.arange(N)[:, None] * frequency[None, :]) % N
    theta = phase * (2.0 * np.pi / N)
    return np.cos(theta), np.sin(theta)


def make_tables():
    cz, sz = angles(False)
    cs, ss = angles(True)
    tz = np.zeros((4, N, 2, 4, M))
    for c in range(4):
        tz[c, :, 0, c, :] = cz
        tz[c, :, 1, c, :] = sz
    tz = tz.reshape(4 * N, 8 * M)
    ty = np.block([[cs.T, -ss.T], [-ss.T, -cs.T]])
    tx = np.zeros((2, M, N, 2))
    tx[0, :, :, 0] = cs.T
    tx[0, :, :, 1] = ss.T
    tx[1, :, :, 0] = -ss.T
    tx[1, :, :, 1] = cs.T
    tx = tx.reshape(2 * M, 2 * N)
    ix = np.zeros((N, 2, 2, M))
    ix[:, 0, 0] = cs
    ix[:, 0, 1] = -ss
    ix[:, 1, 0] = ss
    ix[:, 1, 1] = cs
    ix = ix.reshape(2 * N, 2 * M)
    iy = np.block([[cs, -ss], [ss, cs]])
    iz = np.zeros((2, 4, M, 4, N))
    for c in range(4):
        iz[0, c, :, c, :] = cz.T
        iz[1, c, :, c, :] = -sz.T
    iz = iz.reshape(8 * M, 4 * N)
    expand = np.repeat(np.eye(C), 8, axis=0)
    return {
        "tz": split_np(tz),
        "ty": split_np(ty),
        "tx": split_np(tx),
        "ix": split_np(ix),
        "iy": split_np(iy),
        "iz": split_np(iz),
        "expand": expand.astype(np.float32),
    }


TABLES = make_tables()


def thrice(pair, axis):
    high, low = pair
    return np.concatenate([high, high, low], axis=axis)


TZ = thrice(TABLES["tz"], 0)
TY = np.concatenate(TABLES["ty"], axis=0)
TX = np.concatenate(TABLES["tx"], axis=0)
IX = thrice(TABLES["ix"], 1)
IY = thrice(TABLES["iy"], 1)
IZ = thrice(TABLES["iz"], 0)
EXPAND = TABLES["expand"]


def lane_tables():
    eye = np.eye(M)
    pack = np.zeros((4, N, 4, M))
    unpack = np.zeros((4, M, 4, N))
    copy = np.zeros((4, M, 4, 4, M))
    for q in range(4):
        pack[q, :M, q] = eye
        unpack[q, :, q, :M] = eye
        for h in range(4):
            copy[q, :, q, h] = eye
    pack = pack.reshape(4 * N, N)
    unpack = unpack.reshape(N, 4 * N)
    copy = copy.reshape(N, 4 * N)
    gather = copy.T
    tables = [pack, unpack, copy, gather]
    return [np.concatenate([t, t], axis=0).astype(ml_dtypes.bfloat16) for t in tables]


PACK, UNPACK, COPY, GATHER = lane_tables()


def split(value):
    high = value.astype(BF16)
    low = (value - high.astype(F32)).astype(BF16)
    return high, low


def mm(a, b):
    return jnp.dot(a, b, preferred_element_type=F32)


def move_lanes(data, table):
    high, low = split(data)
    return mm(jnp.concatenate([high, low], axis=1), table[...])


def whole(shape):
    return pl.BlockSpec(shape, lambda *_: (0,) * len(shape))


NQ = 4
AHEAD = 2
GQ = CG // NQ
RQ = 8 * GQ
MESH = pl.DeviceIdType.MESH


def position():
    return lax.axis_index("dp"), lax.axis_index("mp")


def greet():
    dp, mp = position()
    barrier = pltpu.get_barrier_semaphore()

    @pl.loop(1, MP)
    def _(k):
        pl.semaphore_signal(
            barrier, inc=1, device_id=(dp, lax.rem(mp + k, MP)), device_id_type=MESH
        )

    for k in range(1, DP):
        pl.semaphore_signal(
            barrier, inc=1, device_id=(lax.rem(dp + k, DP), mp), device_id_type=MESH
        )


def await_greetings():
    pl.semaphore_wait(pltpu.get_barrier_semaphore(), MP - 1 + DP - 1)


def flat_rows(device, q):
    return pl.ds(pl.multiple_of(device * 64 + q * RQ, 8), RQ)


def piece_rows(q):
    return pl.ds(pl.multiple_of(q * RQ, 8), RQ)


def send_to_modes(q, flat, pieces, send_sem, recv_sem):
    dp, mp = position()

    @pl.loop(1, MP)
    def _(k):
        peer = lax.rem(mp + k, MP)
        pltpu.make_async_remote_copy(
            src_ref=flat.at[flat_rows(peer, q)],
            dst_ref=pieces.at[mp, piece_rows(q)],
            send_sem=send_sem.at[q],
            recv_sem=recv_sem.at[q],
            device_id=(dp, peer),
            device_id_type=MESH,
        ).start()


def send_to_cells(q, pieces, flat, send_sem, recv_sem):
    dp, mp = position()

    @pl.loop(1, MP)
    def _(k):
        peer = lax.rem(mp + k, MP)
        pltpu.make_async_remote_copy(
            src_ref=pieces.at[peer, piece_rows(q)],
            dst_ref=flat.at[flat_rows(mp, q)],
            send_sem=send_sem.at[q],
            recv_sem=recv_sem.at[q],
            device_id=(dp, peer),
            device_id_type=MESH,
        ).start()


def drain_mp(q, flat, sem):
    part = flat.at[pl.ds(0, (MP - 1) * RQ)]
    pltpu.make_async_copy(part, part, sem.at[q]).wait()


def send_dp(q, src, dst, send_sem, recv_sem):
    dp, mp = position()
    groups = pl.ds(q * GQ, GQ)
    for k in range(1, DP):
        peer = lax.rem(dp + k, DP)
        pltpu.make_async_remote_copy(
            src_ref=src.at[peer, groups],
            dst_ref=dst.at[dp, groups],
            send_sem=send_sem.at[q],
            recv_sem=recv_sem.at[q],
            device_id=(peer, mp),
            device_id_type=MESH,
        ).start()


def keep_dp(q, src, dst):
    dp, _ = position()
    groups = pl.ds(q * GQ, GQ)
    dst[dp, groups] = src[dp, groups]


def drain_dp(q, ref, sem):
    part = ref.at[pl.ds(0, DP - 1), pl.ds(0, GQ)]
    pltpu.make_async_copy(part, part, sem.at[q]).wait()


def chunks(body):
    @pl.loop(0, NQ)
    def _(q):
        body(q)


def groups_of(q, body):
    @pl.loop(0, GQ)
    def _(h):
        body(q * GQ + h)


def forward_group(field_ref, g, tz, ty, flat):
    rows = jnp.concatenate([field_ref[4 * g + c].reshape(XL * N, N) for c in range(4)], axis=1)
    high, low = split(rows)
    along_z = mm(jnp.concatenate([high, low, high], axis=1), tz[...])
    stacked = jnp.concatenate(
        [
            jnp.concatenate(
                [along_z[x * N : (x + 1) * N, :N], along_z[x * N : (x + 1) * N, N:]], axis=0
            )
            for x in range(XL)
        ],
        axis=1,
    )
    high, low = split(stacked)
    tables = ty[...]
    both = mm(tables, high)
    tile = both[: 2 * M] + both[2 * M :] + mm(tables[: 2 * M], low)
    for x in range(XL):
        for r in range(2):
            flat[pl.ds(g * 8 + 2 * x + r, M, stride=64), :] = tile[
                r * M : (r + 1) * M, x * N : (x + 1) * N
            ]


def inverse_group(flat, g, iy, iz):
    modes = jnp.concatenate(
        [
            jnp.concatenate(
                [flat[pl.ds(g * 8 + 2 * x + r, M, stride=64), :] for r in range(2)], axis=0
            )
            for x in range(XL)
        ],
        axis=1,
    )
    high, low = split(modes)
    along_y = mm(iy[...], jnp.concatenate([high, low, high], axis=0))
    rows = jnp.concatenate(
        [
            jnp.concatenate(
                [along_y[:N, x * N : (x + 1) * N], along_y[N:, x * N : (x + 1) * N]], axis=1
            )
            for x in range(XL)
        ],
        axis=0,
    )
    high, low = split(rows)
    return mm(jnp.concatenate([high, low, high], axis=1), iz[...])


def chunk_rows(q, h):
    return pl.ds(pl.multiple_of((q * GQ + h) * 8, 8), 8)


def forward_x(pieces, q, tx, out):
    data = jnp.concatenate(
        [pieces[:, chunk_rows(q, h), :].reshape(2 * N, N) for h in range(GQ)], axis=1
    )
    high, low = split(data)
    tables = tx[...]
    both = mm(tables, high)
    tile = both[: 2 * M] + both[2 * M :] + mm(tables[: 2 * M], low)
    for h in range(GQ):
        for d in range(DP):
            for r in range(2):
                out[d, q * GQ + h, r] = tile[
                    r * M + 8 * d : r * M + 8 * d + 8, h * N : (h + 1) * N
                ]


def inverse_x(modes, q, ix, pieces):
    rows = jnp.concatenate(
        [
            jnp.concatenate([modes[:, q * GQ + h, r].reshape(M, N) for r in range(2)], axis=0)
            for h in range(GQ)
        ],
        axis=1,
    )
    high, low = split(rows)
    tile = mm(ix[...], jnp.concatenate([high, low, high], axis=0))
    for h in range(GQ):
        pieces[:, chunk_rows(q, h), :] = tile[:, h * N : (h + 1) * N].reshape(MP, 8, N)


def channel_matrix(matrix, expand, mat):
    spread_cols = lax.dot_general(
        matrix, expand, (((1,), (1,)), ((), ())), precision=lax.Precision.HIGHEST
    )
    full = jnp.dot(expand, spread_cols, precision=lax.Precision.HIGHEST)
    row = lax.broadcasted_iota(jnp.int32, (8 * C, 8 * C), 0)
    col = lax.broadcasted_iota(jnp.int32, (8 * C, 8 * C), 1)
    high, low = split(jnp.where(row % 8 == col % 8, full, 0.0))
    mat[: 8 * C] = high
    mat[8 * C :] = low


YB = 8


def channel_map(in_ref, x, mat, out_ref):
    @pl.loop(0, N // (8 * YB))
    def _(t):
        y = pl.multiple_of(t * 8 * YB, 8)
        data = jnp.concatenate(
            [in_ref[:, x, pl.ds(y + 8 * h, 8), :].reshape(8 * C, N) for h in range(YB)], axis=1
        )
        high, low = split(data)
        tables = mat[...]
        both = mm(tables, high)
        mapped = both[: 8 * C] + both[8 * C :] + mm(tables[: 8 * C], low)
        for h in range(YB):
            out_ref[:, x, pl.ds(y + 8 * h, 8), :] = mapped[:, h * N : (h + 1) * N].reshape(C, 8, N)


def factor_lanes():
    lane = lax.broadcasted_iota(jnp.int32, (8, N), 1)
    return jnp.where(lane % M == 0, 1.0, 2.0).astype(F32) * (1.0 / float(N * N * N))


def mix(spec_ref, w_ref, q, gather, sums, out_ref):
    @pl.loop(0, GQ)
    def _(h):
        for c in range(4):
            o = 4 * (q * GQ + h) + c
            acc = [[None, None] for _ in range(DP)]
            for i in range(CG):
                wr, wi = w_ref[0, i, o], w_ref[1, i, o]
                for b in range(DP):
                    sr, si = spec_ref[b, i, 0], spec_ref[b, i, 1]
                    re = wr * sr - wi * si
                    im = wr * si + wi * sr
                    acc[b] = [re, im] if i == 0 else [acc[b][0] + re, acc[b][1] + im]
            for b in range(DP):
                for r in range(2):
                    at = pl.ds(pl.multiple_of(h * 64 + (2 * b + r) * 8, 8), 8)
                    sums[at, c * N : (c + 1) * N] = acc[b][r]

    mixed = move_lanes(sums[...], gather)
    factor = factor_lanes()
    for h in range(GQ):
        for b in range(DP):
            for r in range(2):
                at = h * 64 + (2 * b + r) * 8
                out_ref[b, q * GQ + h, r] = mixed[at : at + 8] * factor


def spread(grad_ref, copy, rep_ref):
    factor = factor_lanes()
    rows = (grad_ref[...] * factor).reshape(DP * CG * 16, N)
    tiles = move_lanes(rows, copy)
    for b in range(DP):
        for g in range(CG):
            for r in range(2):
                at = ((b * CG + g) * 2 + r) * 8
                for c in range(4):
                    rep_ref[4 * g + c, b, r] = tiles[at : at + 8, c * N : (c + 1) * N]


def back_mix(rep_ref, w_ref, i, out_ref):
    def step(t, acc):
        acc = list(acc)
        for u in range(4):
            o = 4 * t + u
            wr, wi = w_ref[0, i, o], w_ref[1, i, o]
            for b in range(DP):
                gr, gi = rep_ref[o, b, 0], rep_ref[o, b, 1]
                acc[2 * b] = acc[2 * b] + (wr * gr + wi * gi)
                acc[2 * b + 1] = acc[2 * b + 1] + (wr * gi - wi * gr)
        return tuple(acc)

    acc = lax.fori_loop(0, 8, step, tuple(jnp.zeros((8, N), F32) for _ in range(8)))
    for b in range(DP):
        for r in range(2):
            out_ref[b, i, r] = acc[2 * b + r]


def weight_grad(rep_ref, spec_ref, o, out_ref):
    grads = [[rep_ref[o, b, r] for r in range(2)] for b in range(DP)]
    for i in range(CG):
        re = im = None
        for b in range(DP):
            gr, gi = grads[b]
            sr, si = spec_ref[b, i, 0], spec_ref[b, i, 1]
            r1 = gr * sr + gi * si
            i1 = gi * sr - gr * si
            re, im = (r1, i1) if b == 0 else (re + r1, im + i1)
        out_ref[0, i, o] = re
        out_ref[1, i, o] = im


def params(collective_id=None):
    if collective_id is None:
        return pltpu.CompilerParams(vmem_limit_bytes=VMEM_LIMIT)
    return pltpu.CompilerParams(
        vmem_limit_bytes=VMEM_LIMIT, collective_id=collective_id, has_side_effects=True
    )


def in_vmem():
    return pl.BlockSpec(memory_space=pltpu.VMEM)


def anywhere():
    return pl.BlockSpec(memory_space=pl.ANY)


def sems(count):
    return pltpu.SemaphoreType.DMA((count,))


SPEC = (DP, CG, 2, 8, N)
FLAT = (M * 64, N)
PIECES = (MP, 64, N)
CELLS = (C, XL, N, N)
PACKED = (2, CG, C, 8, N)


def to_spectrum(flat, pieces, held, out, tx, mp_sems, dp_sems):
    _, mp = position()

    def body(q):
        drain_mp(q, flat, mp_sems[1])
        pieces[mp, piece_rows(q)] = flat[flat_rows(mp, q)]
        forward_x(pieces, q, tx, held)
        send_dp(q, held, out, *dp_sems)
        keep_dp(q, held, out)

    chunks(body)


def plane_copy(src, dst, sem, x):
    return pltpu.make_async_copy(src.at[:, x], dst.at[:, x], sem.at[x])


def move(q, modes, pieces, flat, ix, mp_sems, dp_recv):
    drain_dp(q, modes, dp_recv)
    inverse_x(modes, q, ix, pieces)
    send_to_cells(q, pieces, flat, *mp_sems)


def exchange_mixed(mix_chunk, mixed, modes, dp_sems):
    def body(q):
        mix_chunk(q)
        send_dp(q, mixed, modes, *dp_sems)
        keep_dp(q, mixed, modes)

    chunks(body)


STAGED = 3


def chunk_copy(src, dst, sem, q):
    part = pl.ds(q * 4 * GQ, 4 * GQ)
    return pltpu.make_async_copy(src.at[part], dst.at[part], sem.at[q])


def group_copy(src, dst, sem, g):
    part = pl.ds(4 * g, 4)
    return pltpu.make_async_copy(src.at[part], dst.at[part], sem.at[g])


def layer_kernel(
    field_ref, w_ref, up_ref, pw_ref, bias_ref, ex_ref,
    tz, ty, tx, ix, iy, iz, pack, gather, copy,
    flat_out, wgrad_out, point_out,
    fields, weight, upstream, cells, packed, rep, mat, sums,
    flat1, pieces1, held1, spectrum, mixed2, modes2, pieces2, flat2,
    flat3, pieces3, held3, grad_spec, mixed4, modes4, pieces4, flat4,
    field_sem, weight_sem, up_sem, point_sem,
    m1_send, m1_recv, d1_send, d1_recv, d2_send, d2_recv, m2_send, m2_recv,
    m3_send, m3_recv, d3_send, d3_recv, d4_send, d4_recv, m4_send, m4_recv,
):
    _, mp = position()
    greet()

    @pl.loop(0, STAGED)
    def _(g):
        group_copy(field_ref, fields, field_sem, g).start()

    def transform(g):
        group_copy(field_ref, fields, field_sem, g).wait()

        @pl.when(g < CG - STAGED)
        def _():
            group_copy(field_ref, fields, field_sem, g + STAGED).start()

        forward_group(fields, g, tz, ty, flat1)

    def field_chunk(q):
        groups_of(q, transform)

        @pl.when(q == 0)
        def _():
            await_greetings()

        send_to_modes(q, flat1, pieces1, m1_send, m1_recv)

    chunks(field_chunk)
    weight_copy = pltpu.make_async_copy(w_ref, weight, weight_sem.at[0])
    weight_copy.start()
    up_copy = pltpu.make_async_copy(up_ref, upstream, up_sem.at[0])
    up_copy.start()
    channel_matrix(pw_ref[...].T, ex_ref[...], mat)

    @pl.loop(0, XL)
    def _(x):
        channel_map(fields, x, mat, cells)

    weight_copy.wait()

    @pl.loop(0, CG)
    def _(g):
        for r in range(2):
            tiles = [
                jnp.pad(weight[r, 4 * g + c].reshape(8 * C, M), ((0, 0), (0, N - M)))
                for c in range(4)
            ]
            packed[r, g] = move_lanes(jnp.concatenate(tiles, axis=1), pack).reshape(C, 8, N)

    to_spectrum(flat1, pieces1, held1, spectrum, tx, (m1_send, m1_recv), (d1_send, d1_recv))
    chunks(lambda q: drain_dp(q, spectrum, d1_recv))

    exchange_mixed(
        lambda q: mix(spectrum, packed, q, gather, sums, mixed2), mixed2, modes2, (d2_send, d2_recv)
    )

    def move_on(q):
        move(q, modes2, pieces2, flat2, ix, (m2_send, m2_recv), d2_recv)

    @pl.loop(0, AHEAD)
    def _(q):
        move_on(q)

        @pl.when(q == 0)
        def _():
            drain_mp(0, flat2, m2_send)

    up_copy.wait()

    def cell_group(g):
        spectral = inverse_group(flat2, g, iy, iz)
        for c in range(4):
            cells[4 * g + c] = (
                cells[4 * g + c]
                + spectral[:, c * N : (c + 1) * N].reshape(XL, N, N)
                + bias_ref[4 * g + c]
            )

        @pl.loop(0, 4 * XL)
        def _(t):
            o, x = 4 * g + t // XL, t % XL
            pre = cells[o, x]
            cdf = 0.5 * (1.0 + lax.erf(pre * np.float32(np.sqrt(0.5))))
            density = jnp.exp(-0.5 * pre * pre) * np.float32(1 / np.sqrt(2 * np.pi))
            cells[o, x] = upstream[o, x].astype(F32) * (cdf + pre * density)

        forward_group(cells, g, tz, ty, flat3)

    def cell_chunk(q):
        drain_mp(q, flat2, m2_recv)
        flat2[flat_rows(mp, q)] = pieces2[mp, piece_rows(q)]

        @pl.loop(0, GQ)
        def _(h):
            cell_group(q * GQ + h)

            @pl.when((h == 0) & (q < NQ - AHEAD))
            def _():
                move_on(q + AHEAD)

        send_to_modes(q, flat3, pieces3, m3_send, m3_recv)

    chunks(cell_chunk)
    to_spectrum(flat3, pieces3, held3, grad_spec, tx, (m3_send, m3_recv), (d3_send, d3_recv))
    chunks(lambda q: drain_dp(q, grad_spec, d3_recv))

    spread(grad_spec, copy, rep)
    exchange_mixed(
        lambda q: groups_of(q, lambda i: back_mix(rep, packed, i, mixed4)),
        mixed4, modes4, (d4_send, d4_recv),
    )
    channel_matrix(pw_ref[...], ex_ref[...], mat)
    chunks(lambda q: move(q, modes4, pieces4, flat4, ix, (m4_send, m4_recv), d4_recv))

    @pl.loop(0, XL)
    def _(x):
        channel_map(cells, x, mat, fields)
        plane_copy(fields, point_out, point_sem, x).start()

    @pl.loop(0, C)
    def _(o):
        weight_grad(rep, spectrum, o, wgrad_out)

    def land(q):
        drain_mp(q, flat4, m4_recv)
        flat4[flat_rows(mp, q)] = pieces4[mp, piece_rows(q)]

    chunks(land)
    flat_out[...] = flat4[...]
    for sem in (d1_send, d2_send, d3_send, d4_send):
        chunks(lambda q, sem=sem: drain_dp(q, mixed4, sem))

    for first, sem in ((0, m1_send), (1, m2_send), (0, m3_send), (0, m4_send)):

        @pl.loop(first, NQ)
        def _(q, sem=sem):
            drain_mp(q, flat4, sem)

    @pl.loop(0, XL)
    def _(x):
        plane_copy(fields, point_out, point_sem, x).wait()


def layer(fields, weight, upstream, point_weight, point_bias):
    tabs = [TZ, TY, TX, IX, IY, IZ, PACK, GATHER, COPY]
    return pl.pallas_call(
        layer_kernel,
        in_specs=[anywhere(), anywhere(), anywhere(), in_vmem()]
        + [pl.BlockSpec(memory_space=pltpu.SMEM)]
        + [in_vmem()] * (1 + len(tabs)),
        out_specs=[in_vmem(), in_vmem(), anywhere()],
        out_shape=[
            jax.ShapeDtypeStruct(FLAT, F32),
            jax.ShapeDtypeStruct(PACKED, F32),
            jax.ShapeDtypeStruct(CELLS, F32),
        ],
        scratch_shapes=[
            pltpu.VMEM(CELLS, F32),
            pltpu.VMEM((2, C, C, 8, M), F32),
            pltpu.VMEM(CELLS, BF16),
            pltpu.VMEM(CELLS, F32),
            pltpu.VMEM(PACKED, F32),
            pltpu.VMEM((C, DP, 2, 8, N), F32),
            pltpu.VMEM((16 * C, 8 * C), BF16),
            pltpu.VMEM((GQ * 64, 4 * N), F32),
        ]
        + 2
        * [
            pltpu.VMEM(FLAT, F32),
            pltpu.VMEM(PIECES, F32),
            pltpu.VMEM(SPEC, F32),
            pltpu.VMEM(SPEC, F32),
            pltpu.VMEM(SPEC, F32),
            pltpu.VMEM(SPEC, F32),
            pltpu.VMEM(PIECES, F32),
            pltpu.VMEM(FLAT, F32),
        ]
        + [sems(CG), sems(1), sems(1), sems(XL)]
        + [sems(NQ)] * 16,
        compiler_params=params(1),
    )(
        fields,
        weight,
        upstream,
        point_weight,
        point_bias,
        jnp.asarray(EXPAND),
        *map(jnp.asarray, tabs),
    )


def finish_kernel(flat, point, wgrad, iy, iz, unpack, cells_out, wgrad_out):
    g = pl.program_id(0)
    spectral = inverse_group(flat, g, iy, iz)
    for c in range(4):
        cells_out[c] = point[c] + spectral[:, c * N : (c + 1) * N].reshape(XL, N, N)

    tiles = move_lanes(wgrad[...].reshape(16 * C, N), unpack)
    for r in range(2):
        for c in range(4):
            wgrad_out[r, c] = tiles[
                r * 8 * C : (r + 1) * 8 * C, c * N : c * N + M
            ].reshape(C, 8, M)


def finish(flat, point, wgrad):
    cell_spec = pl.BlockSpec((4, XL, N, N), lambda g: (g, 0, 0, 0))
    return pl.pallas_call(
        finish_kernel,
        grid=(CG,),
        in_specs=[
            whole(FLAT),
            cell_spec,
            pl.BlockSpec((2, pl.Squeezed(), C, 8, N), lambda g: (0, g, 0, 0, 0)),
            whole(IY.shape),
            whole(IZ.shape),
            whole(UNPACK.shape),
        ],
        out_specs=[cell_spec, pl.BlockSpec((2, 4, C, 8, M), lambda g: (0, g, 0, 0, 0))],
        out_shape=[
            jax.ShapeDtypeStruct(CELLS, F32),
            jax.ShapeDtypeStruct((2, C, C, 8, M), F32),
        ],
        compiler_params=params(),
    )(flat, point, wgrad, *map(jnp.asarray, [IY, IZ, UNPACK]))


def shards(fields, upstream, spectral_weight, point_weight, point_bias):
    flat, wgrad, point = layer(
        fields[0], spectral_weight, upstream[0], point_weight, point_bias
    )
    grad_fields, weight_out = finish(flat, point, wgrad)
    return (grad_fields[None], weight_out)


def solution(mesh):
    placed = (
        P("dp", None, "mp", None, None),
        P("dp", None, "mp", None, None),
        P(None, None, None, "dp", "mp"),
        P(),
        P(),
    )
    return jax.shard_map(
        shards,
        mesh=mesh,
        in_specs=placed,
        out_specs=(P("dp", None, "mp", None, None), P(None, None, None, "dp", "mp")),
        check_vma=False,
    )
```

```python
from functools import partial

import jax
import jax.numpy as jnp
import ml_dtypes
import numpy as np
from jax import lax
from jax.experimental import pallas as pl
from jax.experimental.pallas import tpu as pltpu
from jax.sharding import PartitionSpec as P

N = 128
M = 32
C = 32
XL = 4
CG = 8
DP = 4
MP = 32
F32 = jnp.float32
BF16 = jnp.bfloat16
VMEM_LIMIT = 60 * 1024 * 1024


def split_np(table):
    table = table.astype(np.float32)
    high = table.astype(ml_dtypes.bfloat16)
    low = (table - high.astype(np.float32)).astype(ml_dtypes.bfloat16)
    return high, low


def angles(signed):
    frequency = np.arange(M)
    if signed:
        frequency = np.where(frequency < M // 2, frequency, frequency - M)
    phase = (np.arange(N)[:, None] * frequency[None, :]) % N
    theta = phase * (2.0 * np.pi / N)
    return np.cos(theta), np.sin(theta)


def make_tables():
    cz, sz = angles(False)
    cs, ss = angles(True)
    tz = np.zeros((4, N, 2, 4, M))
    for c in range(4):
        tz[c, :, 0, c, :] = cz
        tz[c, :, 1, c, :] = sz
    tz = tz.reshape(4 * N, 8 * M)
    ty = np.block([[cs.T, -ss.T], [-ss.T, -cs.T]])
    tx = np.zeros((2, M, N, 2))
    tx[0, :, :, 0] = cs.T
    tx[0, :, :, 1] = ss.T
    tx[1, :, :, 0] = -ss.T
    tx[1, :, :, 1] = cs.T
    tx = tx.reshape(2 * M, 2 * N)
    ix = np.zeros((N, 2, 2, M))
    ix[:, 0, 0] = cs
    ix[:, 0, 1] = -ss
    ix[:, 1, 0] = ss
    ix[:, 1, 1] = cs
    ix = ix.reshape(2 * N, 2 * M)
    iy = np.block([[cs, -ss], [ss, cs]])
    iz = np.zeros((2, 4, M, 4, N))
    for c in range(4):
        iz[0, c, :, c, :] = cz.T
        iz[1, c, :, c, :] = -sz.T
    iz = iz.reshape(8 * M, 4 * N)
    expand = np.repeat(np.eye(C), 8, axis=0)
    return {
        "tz": split_np(tz),
        "ty": split_np(ty),
        "tx": split_np(tx),
        "ix": split_np(ix),
        "iy": split_np(iy),
        "iz": split_np(iz),
        "expand": expand.astype(np.float32),
    }


TABLES = make_tables()


def thrice(pair, axis):
    high, low = pair
    return np.concatenate([high, high, low], axis=axis)


TZ = thrice(TABLES["tz"], 0)
TY = np.concatenate(TABLES["ty"], axis=0)
TX = np.concatenate(TABLES["tx"], axis=0)
IX = thrice(TABLES["ix"], 1)
IY = thrice(TABLES["iy"], 1)
IZ = thrice(TABLES["iz"], 0)
EXPAND = TABLES["expand"]


def lane_tables():
    eye = np.eye(M)
    pack = np.zeros((4, N, 4, M))
    unpack = np.zeros((4, M, 4, N))
    copy = np.zeros((4, M, 4, 4, M))
    for q in range(4):
        pack[q, :M, q] = eye
        unpack[q, :, q, :M] = eye
        for h in range(4):
            copy[q, :, q, h] = eye
    pack = pack.reshape(4 * N, N)
    unpack = unpack.reshape(N, 4 * N)
    copy = copy.reshape(N, 4 * N)
    gather = copy.T
    tables = [pack, unpack, copy, gather]
    return [np.concatenate([t, t], axis=0).astype(ml_dtypes.bfloat16) for t in tables]


PACK, UNPACK, COPY, GATHER = lane_tables()


def split(value):
    high = value.astype(BF16)
    low = (value - high.astype(F32)).astype(BF16)
    return high, low


def mm(a, b):
    return jnp.dot(a, b, preferred_element_type=F32)


def move_lanes(data, table):
    high, low = split(data)
    return mm(jnp.concatenate([high, low], axis=1), table[...])


def whole(shape):
    return pl.BlockSpec(shape, lambda *_: (0,) * len(shape))


NQ = 4
LEFT = 1
AHEAD = 4
GQ = CG // NQ
RQ = 8 * GQ
MESH = pl.DeviceIdType.MESH


def position():
    return lax.axis_index("dp"), lax.axis_index("mp")


def greet():
    dp, mp = position()
    barrier = pltpu.get_barrier_semaphore()

    @pl.loop(1, MP)
    def _(k):
        pl.semaphore_signal(
            barrier, inc=1, device_id=(dp, lax.rem(mp + k, MP)), device_id_type=MESH
        )

    for k in range(1, DP):
        pl.semaphore_signal(
            barrier, inc=1, device_id=(lax.rem(dp + k, DP), mp), device_id_type=MESH
        )


def await_greetings():
    pl.semaphore_wait(pltpu.get_barrier_semaphore(), MP - 1 + DP - 1)


def flat_rows(device, q):
    return pl.ds(pl.multiple_of(device * 64 + q * RQ, 8), RQ)


def piece_rows(q):
    return pl.ds(pl.multiple_of(q * RQ, 8), RQ)


def send_to_modes(q, flat, pieces, send_sem, recv_sem):
    dp, mp = position()

    @pl.loop(1, MP)
    def _(k):
        peer = lax.rem(mp + k, MP)
        pltpu.make_async_remote_copy(
            src_ref=flat.at[flat_rows(peer, q)],
            dst_ref=pieces.at[mp, piece_rows(q)],
            send_sem=send_sem.at[q],
            recv_sem=recv_sem.at[q],
            device_id=(dp, peer),
            device_id_type=MESH,
        ).start()


def send_to_cells(q, pieces, flat, send_sem, recv_sem):
    dp, mp = position()

    @pl.loop(1, MP)
    def _(k):
        peer = lax.rem(mp + k, MP)
        pltpu.make_async_remote_copy(
            src_ref=pieces.at[peer, piece_rows(q)],
            dst_ref=flat.at[flat_rows(mp, q)],
            send_sem=send_sem.at[q],
            recv_sem=recv_sem.at[q],
            device_id=(dp, peer),
            device_id_type=MESH,
        ).start()


def drain_mp(q, flat, sem):
    part = flat.at[pl.ds(0, (MP - 1) * RQ)]
    pltpu.make_async_copy(part, part, sem.at[q]).wait()


def send_dp(q, src, dst, send_sem, recv_sem):
    dp, mp = position()
    groups = pl.ds(q * GQ, GQ)
    for k in range(1, DP):
        peer = lax.rem(dp + k, DP)
        pltpu.make_async_remote_copy(
            src_ref=src.at[peer, groups],
            dst_ref=dst.at[dp, groups],
            send_sem=send_sem.at[q],
            recv_sem=recv_sem.at[q],
            device_id=(peer, mp),
            device_id_type=MESH,
        ).start()


def keep_dp(q, src, dst):
    dp, _ = position()
    groups = pl.ds(q * GQ, GQ)
    dst[dp, groups] = src[dp, groups]


def drain_dp(q, ref, sem):
    part = ref.at[pl.ds(0, DP - 1), pl.ds(0, GQ)]
    pltpu.make_async_copy(part, part, sem.at[q]).wait()


def chunks(body):
    @pl.loop(0, NQ)
    def _(q):
        body(q)


def groups_of(q, body):
    @pl.loop(0, GQ)
    def _(h):
        body(q * GQ + h)


def forward_group(field_ref, g, tz, ty, flat):
    rows = jnp.concatenate([field_ref[4 * g + c].reshape(XL * N, N) for c in range(4)], axis=1)
    high, low = split(rows)
    along_z = mm(jnp.concatenate([high, low, high], axis=1), tz[...])
    stacked = jnp.concatenate(
        [
            jnp.concatenate(
                [along_z[x * N : (x + 1) * N, :N], along_z[x * N : (x + 1) * N, N:]], axis=0
            )
            for x in range(XL)
        ],
        axis=1,
    )
    high, low = split(stacked)
    tables = ty[...]
    both = mm(tables, high)
    tile = both[: 2 * M] + both[2 * M :] + mm(tables[: 2 * M], low)
    for x in range(XL):
        for r in range(2):
            flat[pl.ds(g * 8 + 2 * x + r, M, stride=64), :] = tile[
                r * M : (r + 1) * M, x * N : (x + 1) * N
            ]


def inverse_group(flat, g, iy, iz):
    modes = jnp.concatenate(
        [
            jnp.concatenate(
                [flat[pl.ds(g * 8 + 2 * x + r, M, stride=64), :] for r in range(2)], axis=0
            )
            for x in range(XL)
        ],
        axis=1,
    )
    high, low = split(modes)
    along_y = mm(iy[...], jnp.concatenate([high, low, high], axis=0))
    rows = jnp.concatenate(
        [
            jnp.concatenate(
                [along_y[:N, x * N : (x + 1) * N], along_y[N:, x * N : (x + 1) * N]], axis=1
            )
            for x in range(XL)
        ],
        axis=0,
    )
    high, low = split(rows)
    return mm(jnp.concatenate([high, low, high], axis=1), iz[...])


def chunk_rows(q, h):
    return pl.ds(pl.multiple_of((q * GQ + h) * 8, 8), 8)


def forward_x(pieces, q, tx, out):
    data = jnp.concatenate(
        [pieces[:, chunk_rows(q, h), :].reshape(2 * N, N) for h in range(GQ)], axis=1
    )
    high, low = split(data)
    tables = tx[...]
    both = mm(tables, high)
    tile = both[: 2 * M] + both[2 * M :] + mm(tables[: 2 * M], low)
    for h in range(GQ):
        for d in range(DP):
            for r in range(2):
                out[d, q * GQ + h, r] = tile[
                    r * M + 8 * d : r * M + 8 * d + 8, h * N : (h + 1) * N
                ]


def inverse_x(modes, q, ix, pieces):
    rows = jnp.concatenate(
        [
            jnp.concatenate([modes[:, q * GQ + h, r].reshape(M, N) for r in range(2)], axis=0)
            for h in range(GQ)
        ],
        axis=1,
    )
    high, low = split(rows)
    tile = mm(ix[...], jnp.concatenate([high, low, high], axis=0))
    for h in range(GQ):
        pieces[:, chunk_rows(q, h), :] = tile[:, h * N : (h + 1) * N].reshape(MP, 8, N)


def channel_matrix(matrix, expand, mat):
    spread_cols = lax.dot_general(
        matrix, expand, (((1,), (1,)), ((), ())), precision=lax.Precision.HIGHEST
    )
    full = jnp.dot(expand, spread_cols, precision=lax.Precision.HIGHEST)
    row = lax.broadcasted_iota(jnp.int32, (8 * C, 8 * C), 0)
    col = lax.broadcasted_iota(jnp.int32, (8 * C, 8 * C), 1)
    high, low = split(jnp.where(row % 8 == col % 8, full, 0.0))
    mat[: 8 * C] = high
    mat[8 * C :] = low


YB = 8


def channel_map(in_ref, x, mat, out_ref):
    @pl.loop(0, N // (8 * YB))
    def _(t):
        y = pl.multiple_of(t * 8 * YB, 8)
        data = jnp.concatenate(
            [in_ref[:, x, pl.ds(y + 8 * h, 8), :].reshape(8 * C, N) for h in range(YB)], axis=1
        )
        high, low = split(data)
        tables = mat[...]
        both = mm(tables, high)
        mapped = both[: 8 * C] + both[8 * C :] + mm(tables[: 8 * C], low)
        for h in range(YB):
            out_ref[:, x, pl.ds(y + 8 * h, 8), :] = mapped[:, h * N : (h + 1) * N].reshape(C, 8, N)


def factor_lanes():
    lane = lax.broadcasted_iota(jnp.int32, (8, N), 1)
    return jnp.where(lane % M == 0, 1.0, 2.0).astype(F32) * (1.0 / float(N * N * N))


def mix(spec_ref, w_ref, q, gather, sums, out_ref):
    @pl.loop(0, GQ)
    def _(h):
        for c in range(4):
            o = 4 * (q * GQ + h) + c
            acc = [[None, None] for _ in range(DP)]
            for i in range(CG):
                wr, wi = w_ref[0, i, o], w_ref[1, i, o]
                for b in range(DP):
                    sr, si = spec_ref[b, i, 0], spec_ref[b, i, 1]
                    re = wr * sr - wi * si
                    im = wr * si + wi * sr
                    acc[b] = [re, im] if i == 0 else [acc[b][0] + re, acc[b][1] + im]
            for b in range(DP):
                for r in range(2):
                    at = pl.ds(pl.multiple_of(h * 64 + (2 * b + r) * 8, 8), 8)
                    sums[at, c * N : (c + 1) * N] = acc[b][r]

    mixed = move_lanes(sums[...], gather)
    factor = factor_lanes()
    for h in range(GQ):
        for b in range(DP):
            for r in range(2):
                at = h * 64 + (2 * b + r) * 8
                out_ref[b, q * GQ + h, r] = mixed[at : at + 8] * factor


def spread(grad_ref, copy, rep_ref):
    factor = factor_lanes()
    rows = (grad_ref[...] * factor).reshape(DP * CG * 16, N)
    tiles = move_lanes(rows, copy)
    for b in range(DP):
        for g in range(CG):
            for r in range(2):
                at = ((b * CG + g) * 2 + r) * 8
                for c in range(4):
                    rep_ref[4 * g + c, b, r] = tiles[at : at + 8, c * N : (c + 1) * N]


def back_mix(rep_ref, w_ref, i, out_ref):
    def step(t, acc):
        acc = list(acc)
        for u in range(4):
            o = 4 * t + u
            wr, wi = w_ref[0, i, o], w_ref[1, i, o]
            for b in range(DP):
                gr, gi = rep_ref[o, b, 0], rep_ref[o, b, 1]
                acc[2 * b] = acc[2 * b] + (wr * gr + wi * gi)
                acc[2 * b + 1] = acc[2 * b + 1] + (wr * gi - wi * gr)
        return tuple(acc)

    acc = lax.fori_loop(0, 8, step, tuple(jnp.zeros((8, N), F32) for _ in range(8)))
    for b in range(DP):
        for r in range(2):
            out_ref[b, i, r] = acc[2 * b + r]


def weight_grad(rep_ref, spec_ref, o, out_ref):
    grads = [[rep_ref[o, b, r] for r in range(2)] for b in range(DP)]
    for i in range(CG):
        re = im = None
        for b in range(DP):
            gr, gi = grads[b]
            sr, si = spec_ref[b, i, 0], spec_ref[b, i, 1]
            r1 = gr * sr + gi * si
            i1 = gi * sr - gr * si
            re, im = (r1, i1) if b == 0 else (re + r1, im + i1)
        out_ref[0, i, o] = re
        out_ref[1, i, o] = im


def params(collective_id=None):
    if collective_id is None:
        return pltpu.CompilerParams(vmem_limit_bytes=VMEM_LIMIT)
    return pltpu.CompilerParams(
        vmem_limit_bytes=VMEM_LIMIT, collective_id=collective_id, has_side_effects=True
    )


def in_vmem():
    return pl.BlockSpec(memory_space=pltpu.VMEM)


def anywhere():
    return pl.BlockSpec(memory_space=pl.ANY)


def sems(count):
    return pltpu.SemaphoreType.DMA((count,))


SPEC = (DP, CG, 2, 8, N)
FLAT = (M * 64, N)
PIECES = (MP, 64, N)
CELLS = (C, XL, N, N)
PACKED = (2, CG, C, 8, N)


def to_spectrum(flat, pieces, held, out, tx, mp_sems, dp_sems):
    _, mp = position()

    def body(q):
        drain_mp(q, flat, mp_sems[1])
        pieces[mp, piece_rows(q)] = flat[flat_rows(mp, q)]
        forward_x(pieces, q, tx, held)
        send_dp(q, held, out, *dp_sems)
        keep_dp(q, held, out)

    chunks(body)


def move(q, modes, pieces, flat, ix, mp_sems, dp_recv):
    drain_dp(q, modes, dp_recv)
    inverse_x(modes, q, ix, pieces)
    send_to_cells(q, pieces, flat, *mp_sems)


def exchange_mixed(mix_chunk, mixed, modes, dp_sems):
    def body(q):
        mix_chunk(q)
        send_dp(q, mixed, modes, *dp_sems)
        keep_dp(q, mixed, modes)

    chunks(body)


STAGED = 3


def chunk_copy(src, dst, sem, q):
    part = pl.ds(q * 4 * GQ, 4 * GQ)
    return pltpu.make_async_copy(src.at[part], dst.at[part], sem.at[q])


def group_copy(src, dst, sem, g):
    part = pl.ds(4 * g, 4)
    return pltpu.make_async_copy(src.at[part], dst.at[part], sem.at[g])


def add_spectral(flat, g, iy, iz, cells):
    spectral = inverse_group(flat, g, iy, iz)
    for c in range(4):
        cells[4 * g + c] = cells[4 * g + c] + spectral[:, c * N : (c + 1) * N].reshape(XL, N, N)


def layer_kernel(
    field_ref, w_ref, up_ref, pw_ref, bias_ref, ex_ref,
    tz, ty, tx, ix, iy, iz, pack, gather, copy,
    flat_out, wgrad_out, point_out,
    fields, weight, upstream, cells, packed, rep, mat, sums,
    flat1, pieces1, held1, spectrum, mixed2, modes2, pieces2, flat2,
    flat3, pieces3, held3, grad_spec, mixed4, modes4, pieces4, flat4,
    field_sem, weight_sem, up_sem, point_sem,
    m1_send, m1_recv, d1_send, d1_recv, d2_send, d2_recv, m2_send, m2_recv,
    m3_send, m3_recv, d3_send, d3_recv, d4_send, d4_recv, m4_send, m4_recv,
):
    _, mp = position()
    greet()

    @pl.loop(0, STAGED)
    def _(g):
        group_copy(field_ref, fields, field_sem, g).start()

    def weight_copy(g):
        part = pl.ds(4 * g, 4)
        return pltpu.make_async_copy(w_ref.at[:, part], weight.at[:, part], weight_sem.at[g])

    def transform(g):
        weight_copy(g).start()
        group_copy(field_ref, fields, field_sem, g).wait()

        @pl.when(g < CG - STAGED)
        def _():
            group_copy(field_ref, fields, field_sem, g + STAGED).start()

        forward_group(fields, g, tz, ty, flat1)

    def field_chunk(q):
        groups_of(q, transform)

        @pl.when(q == 0)
        def _():
            await_greetings()

        send_to_modes(q, flat1, pieces1, m1_send, m1_recv)

    chunks(field_chunk)
    up_copy = pltpu.make_async_copy(up_ref, upstream, up_sem.at[0])
    up_copy.start()
    channel_matrix(pw_ref[...].T, ex_ref[...], mat)
    @pl.loop(0, CG)
    def _(g):
        weight_copy(g).wait()
        for r in range(2):
            tiles = [
                jnp.pad(weight[r, 4 * g + c].reshape(8 * C, M), ((0, 0), (0, N - M)))
                for c in range(4)
            ]
            packed[r, g] = move_lanes(jnp.concatenate(tiles, axis=1), pack).reshape(C, 8, N)

    to_spectrum(flat1, pieces1, held1, spectrum, tx, (m1_send, m1_recv), (d1_send, d1_recv))
    chunks(lambda q: drain_dp(q, spectrum, d1_recv))

    exchange_mixed(
        lambda q: mix(spectrum, packed, q, gather, sums, mixed2), mixed2, modes2, (d2_send, d2_recv)
    )

    def move_on(q):
        move(q, modes2, pieces2, flat2, ix, (m2_send, m2_recv), d2_recv)

    @pl.loop(0, AHEAD)
    def _(q):
        move_on(q)

    @pl.loop(0, XL)
    def _(x):
        channel_map(fields, x, mat, cells)

    up_copy.wait()

    def cell_group(g):
        spectral = inverse_group(flat2, g, iy, iz)
        for c in range(4):
            cells[4 * g + c] = (
                cells[4 * g + c]
                + spectral[:, c * N : (c + 1) * N].reshape(XL, N, N)
                + bias_ref[4 * g + c]
            )

        @pl.loop(0, 4 * XL)
        def _(t):
            o, x = 4 * g + t // XL, t % XL
            pre = cells[o, x]
            cdf = 0.5 * (1.0 + lax.erf(pre * np.float32(np.sqrt(0.5))))
            density = jnp.exp(-0.5 * pre * pre) * np.float32(1 / np.sqrt(2 * np.pi))
            cells[o, x] = upstream[o, x].astype(F32) * (cdf + pre * density)

        forward_group(cells, g, tz, ty, flat3)

    def cell_chunk(q):
        drain_mp(q, flat2, m2_recv)
        flat2[flat_rows(mp, q)] = pieces2[mp, piece_rows(q)]

        @pl.loop(0, GQ)
        def _(h):
            cell_group(q * GQ + h)

            @pl.when((h == 0) & (q < NQ - AHEAD))
            def _():
                move_on(q + AHEAD)

        send_to_modes(q, flat3, pieces3, m3_send, m3_recv)

    chunks(cell_chunk)
    channel_matrix(pw_ref[...], ex_ref[...], mat)
    to_spectrum(flat3, pieces3, held3, grad_spec, tx, (m3_send, m3_recv), (d3_send, d3_recv))
    chunks(lambda q: drain_dp(q, grad_spec, d3_recv))

    spread(grad_spec, copy, rep)
    exchange_mixed(
        lambda q: groups_of(q, lambda i: back_mix(rep, packed, i, mixed4)),
        mixed4, modes4, (d4_send, d4_recv),
    )

    def move_back(q):
        move(q, modes4, pieces4, flat4, ix, (m4_send, m4_recv), d4_recv)
        channel_map(cells, q, mat, fields)

    chunks(move_back)

    @pl.loop(0, C)
    def _(o):
        weight_grad(rep, spectrum, o, wgrad_out)

    def land(q):
        drain_mp(q, flat4, m4_recv)
        flat4[flat_rows(mp, q)] = pieces4[mp, piece_rows(q)]

        @pl.when(q < NQ - LEFT)
        def _():
            groups_of(q, lambda g: add_spectral(flat4, g, iy, iz, fields))

        chunk_copy(fields, point_out, point_sem, q).start()

    chunks(land)
    flat_out[...] = flat4[...]
    for sem in (d1_send, d2_send, d3_send, d4_send):
        chunks(lambda q, sem=sem: drain_dp(q, mixed4, sem))

    for first, sem in ((0, m1_send), (0, m2_send), (0, m3_send), (0, m4_send)):

        @pl.loop(first, NQ)
        def _(q, sem=sem):
            drain_mp(q, flat4, sem)

    chunks(lambda q: chunk_copy(fields, point_out, point_sem, q).wait())


def layer(fields, weight, upstream, point_weight, point_bias):
    tabs = [TZ, TY, TX, IX, IY, IZ, PACK, GATHER, COPY]
    return pl.pallas_call(
        layer_kernel,
        in_specs=[anywhere(), anywhere(), anywhere(), in_vmem()]
        + [pl.BlockSpec(memory_space=pltpu.SMEM)]
        + [in_vmem()] * (1 + len(tabs)),
        out_specs=[in_vmem(), in_vmem(), anywhere()],
        out_shape=[
            jax.ShapeDtypeStruct(FLAT, F32),
            jax.ShapeDtypeStruct(PACKED, F32),
            jax.ShapeDtypeStruct(CELLS, F32),
        ],
        scratch_shapes=[
            pltpu.VMEM(CELLS, F32),
            pltpu.VMEM((2, C, C, 8, M), F32),
            pltpu.VMEM(CELLS, BF16),
            pltpu.VMEM(CELLS, F32),
            pltpu.VMEM(PACKED, F32),
            pltpu.VMEM((C, DP, 2, 8, N), F32),
            pltpu.VMEM((16 * C, 8 * C), BF16),
            pltpu.VMEM((GQ * 64, 4 * N), F32),
        ]
        + 2
        * [
            pltpu.VMEM(FLAT, F32),
            pltpu.VMEM(PIECES, F32),
            pltpu.VMEM(SPEC, F32),
            pltpu.VMEM(SPEC, F32),
            pltpu.VMEM(SPEC, F32),
            pltpu.VMEM(SPEC, F32),
            pltpu.VMEM(PIECES, F32),
            pltpu.VMEM(FLAT, F32),
        ]
        + [sems(CG), sems(CG), sems(1), sems(NQ)]
        + [sems(NQ)] * 16,
        compiler_params=params(1),
    )(
        fields,
        weight,
        upstream,
        point_weight,
        point_bias,
        jnp.asarray(EXPAND),
        *map(jnp.asarray, tabs),
    )


def finish_kernel(flat, point, wgrad, iy, iz, unpack, cells_out, wgrad_out):
    g = pl.program_id(0)

    @pl.when(g < CG - LEFT * GQ)
    def _():
        cells_out[...] = point[...]

    @pl.when(g >= CG - LEFT * GQ)
    def _():
        spectral = inverse_group(flat, g, iy, iz)
        for c in range(4):
            cells_out[c] = point[c] + spectral[:, c * N : (c + 1) * N].reshape(XL, N, N)

    tiles = move_lanes(wgrad[...].reshape(16 * C, N), unpack)
    for r in range(2):
        for c in range(4):
            wgrad_out[r, c] = tiles[
                r * 8 * C : (r + 1) * 8 * C, c * N : c * N + M
            ].reshape(C, 8, M)


def finish(flat, point, wgrad):
    cell_spec = pl.BlockSpec((4, XL, N, N), lambda g: (g, 0, 0, 0))
    return pl.pallas_call(
        finish_kernel,
        grid=(CG,),
        in_specs=[
            whole(FLAT),
            cell_spec,
            pl.BlockSpec((2, pl.Squeezed(), C, 8, N), lambda g: (0, g, 0, 0, 0)),
            whole(IY.shape),
            whole(IZ.shape),
            whole(UNPACK.shape),
        ],
        out_specs=[cell_spec, pl.BlockSpec((2, 4, C, 8, M), lambda g: (0, g, 0, 0, 0))],
        out_shape=[
            jax.ShapeDtypeStruct(CELLS, F32),
            jax.ShapeDtypeStruct((2, C, C, 8, M), F32),
        ],
        compiler_params=params(),
    )(flat, point, wgrad, *map(jnp.asarray, [IY, IZ, UNPACK]))


def shards(fields, upstream, spectral_weight, point_weight, point_bias):
    flat, wgrad, point = layer(
        fields[0], spectral_weight, upstream[0], point_weight, point_bias
    )
    grad_fields, weight_out = finish(flat, point, wgrad)
    return (grad_fields[None], weight_out)


def solution(mesh):
    placed = (
        P("dp", None, "mp", None, None),
        P("dp", None, "mp", None, None),
        P(None, None, None, "dp", "mp"),
        P(),
        P(),
    )
    return jax.shard_map(
        shards,
        mesh=mesh,
        in_specs=placed,
        out_specs=(P("dp", None, "mp", None, None), P(None, None, None, "dp", "mp")),
        check_vma=False,
    )
```

```python
from functools import partial

import jax
import jax.numpy as jnp
import ml_dtypes
import numpy as np
from jax import lax
from jax.experimental import pallas as pl
from jax.experimental.pallas import tpu as pltpu
from jax.sharding import PartitionSpec as P

N = 128
M = 32
C = 32
XL = 4
CG = 8
DP = 4
MP = 32
F32 = jnp.float32
BF16 = jnp.bfloat16
VMEM_LIMIT = 60 * 1024 * 1024


def split_np(table):
    table = table.astype(np.float32)
    high = table.astype(ml_dtypes.bfloat16)
    low = (table - high.astype(np.float32)).astype(ml_dtypes.bfloat16)
    return high, low


def angles(signed):
    frequency = np.arange(M)
    if signed:
        frequency = np.where(frequency < M // 2, frequency, frequency - M)
    phase = (np.arange(N)[:, None] * frequency[None, :]) % N
    theta = phase * (2.0 * np.pi / N)
    return np.cos(theta), np.sin(theta)


def make_tables():
    cz, sz = angles(False)
    cs, ss = angles(True)
    tz = np.zeros((4, N, 2, 4, M))
    for c in range(4):
        tz[c, :, 0, c, :] = cz
        tz[c, :, 1, c, :] = sz
    tz = tz.reshape(4 * N, 8 * M)
    ty = np.block([[cs.T, -ss.T], [-ss.T, -cs.T]])
    tx = np.zeros((2, M, N, 2))
    tx[0, :, :, 0] = cs.T
    tx[0, :, :, 1] = ss.T
    tx[1, :, :, 0] = -ss.T
    tx[1, :, :, 1] = cs.T
    tx = tx.reshape(2 * M, 2 * N)
    ix = np.zeros((N, 2, 2, M))
    ix[:, 0, 0] = cs
    ix[:, 0, 1] = -ss
    ix[:, 1, 0] = ss
    ix[:, 1, 1] = cs
    ix = ix.reshape(2 * N, 2 * M)
    iy = np.block([[cs, -ss], [ss, cs]])
    iz = np.zeros((2, 4, M, 4, N))
    for c in range(4):
        iz[0, c, :, c, :] = cz.T
        iz[1, c, :, c, :] = -sz.T
    iz = iz.reshape(8 * M, 4 * N)
    expand = np.repeat(np.eye(C), 8, axis=0)
    return {
        "tz": split_np(tz),
        "ty": split_np(ty),
        "tx": split_np(tx),
        "ix": split_np(ix),
        "iy": split_np(iy),
        "iz": split_np(iz),
        "expand": expand.astype(np.float32),
    }


TABLES = make_tables()


def thrice(pair, axis):
    high, low = pair
    return np.concatenate([high, high, low], axis=axis)


TZ = thrice(TABLES["tz"], 0)
TY = np.concatenate(TABLES["ty"], axis=0)
TX = np.concatenate(TABLES["tx"], axis=0)
IX = thrice(TABLES["ix"], 1)
IY = thrice(TABLES["iy"], 1)
IZ = thrice(TABLES["iz"], 0)
EXPAND = TABLES["expand"]


def lane_tables():
    eye = np.eye(M)
    pack = np.zeros((4, N, 4, M))
    unpack = np.zeros((4, M, 4, N))
    copy = np.zeros((4, M, 4, 4, M))
    for q in range(4):
        pack[q, :M, q] = eye
        unpack[q, :, q, :M] = eye
        for h in range(4):
            copy[q, :, q, h] = eye
    pack = pack.reshape(4 * N, N)
    unpack = unpack.reshape(N, 4 * N)
    copy = copy.reshape(N, 4 * N)
    gather = copy.T
    tables = [pack, unpack, copy, gather]
    return [np.concatenate([t, t], axis=0).astype(ml_dtypes.bfloat16) for t in tables]


PACK, UNPACK, COPY, GATHER = lane_tables()


def split(value):
    high = value.astype(BF16)
    low = (value - high.astype(F32)).astype(BF16)
    return high, low


def mm(a, b):
    return jnp.dot(a, b, preferred_element_type=F32)


def move_lanes(data, table):
    high, low = split(data)
    return mm(jnp.concatenate([high, low], axis=1), table[...])


def whole(shape):
    return pl.BlockSpec(shape, lambda *_: (0,) * len(shape))


NQ = 4
LEFT = 1
AHEAD = 4
GQ = CG // NQ
RQ = 8 * GQ
MESH = pl.DeviceIdType.MESH


def position():
    return lax.axis_index("dp"), lax.axis_index("mp")


def greet():
    dp, mp = position()
    barrier = pltpu.get_barrier_semaphore()

    @pl.loop(1, MP)
    def _(k):
        pl.semaphore_signal(
            barrier, inc=1, device_id=(dp, lax.rem(mp + k, MP)), device_id_type=MESH
        )

    for k in range(1, DP):
        pl.semaphore_signal(
            barrier, inc=1, device_id=(lax.rem(dp + k, DP), mp), device_id_type=MESH
        )


def await_greetings():
    pl.semaphore_wait(pltpu.get_barrier_semaphore(), MP - 1 + DP - 1)


def flat_rows(device, q):
    return pl.ds(pl.multiple_of(device * 64 + q * RQ, 8), RQ)


def piece_rows(q):
    return pl.ds(pl.multiple_of(q * RQ, 8), RQ)


def send_to_modes(q, flat, pieces, send_sem, recv_sem):
    dp, mp = position()

    @pl.loop(1, MP)
    def _(k):
        peer = lax.rem(mp + k, MP)
        pltpu.make_async_remote_copy(
            src_ref=flat.at[flat_rows(peer, q)],
            dst_ref=pieces.at[mp, piece_rows(q)],
            send_sem=send_sem.at[q],
            recv_sem=recv_sem.at[q],
            device_id=(dp, peer),
            device_id_type=MESH,
        ).start()


def send_to_cells(q, pieces, flat, send_sem, recv_sem):
    dp, mp = position()

    @pl.loop(1, MP)
    def _(k):
        peer = lax.rem(mp + k, MP)
        pltpu.make_async_remote_copy(
            src_ref=pieces.at[peer, piece_rows(q)],
            dst_ref=flat.at[flat_rows(mp, q)],
            send_sem=send_sem.at[q],
            recv_sem=recv_sem.at[q],
            device_id=(dp, peer),
            device_id_type=MESH,
        ).start()


def drain_mp(q, flat, sem):
    part = flat.at[pl.ds(0, (MP - 1) * RQ)]
    pltpu.make_async_copy(part, part, sem.at[q]).wait()


def send_dp(q, src, dst, send_sem, recv_sem):
    dp, mp = position()
    groups = pl.ds(q * GQ, GQ)
    for k in range(1, DP):
        peer = lax.rem(dp + k, DP)
        pltpu.make_async_remote_copy(
            src_ref=src.at[peer, groups],
            dst_ref=dst.at[dp, groups],
            send_sem=send_sem.at[q],
            recv_sem=recv_sem.at[q],
            device_id=(peer, mp),
            device_id_type=MESH,
        ).start()


def keep_dp(q, src, dst):
    dp, _ = position()
    groups = pl.ds(q * GQ, GQ)
    dst[dp, groups] = src[dp, groups]


def drain_dp(q, ref, sem):
    part = ref.at[pl.ds(0, DP - 1), pl.ds(0, GQ)]
    pltpu.make_async_copy(part, part, sem.at[q]).wait()


def chunks(body):
    @pl.loop(0, NQ)
    def _(q):
        body(q)


def groups_of(q, body):
    @pl.loop(0, GQ)
    def _(h):
        body(q * GQ + h)


def forward_group(field_ref, g, tz, ty, flat):
    rows = jnp.concatenate([field_ref[4 * g + c].reshape(XL * N, N) for c in range(4)], axis=1)
    high, low = split(rows)
    along_z = mm(jnp.concatenate([high, low, high], axis=1), tz[...])
    stacked = jnp.concatenate(
        [
            jnp.concatenate(
                [along_z[x * N : (x + 1) * N, :N], along_z[x * N : (x + 1) * N, N:]], axis=0
            )
            for x in range(XL)
        ],
        axis=1,
    )
    high, low = split(stacked)
    tables = ty[...]
    both = mm(tables, high)
    tile = both[: 2 * M] + both[2 * M :] + mm(tables[: 2 * M], low)
    for x in range(XL):
        for r in range(2):
            flat[pl.ds(g * 8 + 2 * x + r, M, stride=64), :] = tile[
                r * M : (r + 1) * M, x * N : (x + 1) * N
            ]


def inverse_group(flat, g, iy, iz):
    modes = jnp.concatenate(
        [
            jnp.concatenate(
                [flat[pl.ds(g * 8 + 2 * x + r, M, stride=64), :] for r in range(2)], axis=0
            )
            for x in range(XL)
        ],
        axis=1,
    )
    high, low = split(modes)
    along_y = mm(iy[...], jnp.concatenate([high, low, high], axis=0))
    rows = jnp.concatenate(
        [
            jnp.concatenate(
                [along_y[:N, x * N : (x + 1) * N], along_y[N:, x * N : (x + 1) * N]], axis=1
            )
            for x in range(XL)
        ],
        axis=0,
    )
    high, low = split(rows)
    return mm(jnp.concatenate([high, low, high], axis=1), iz[...])


def chunk_rows(q, h):
    return pl.ds(pl.multiple_of((q * GQ + h) * 8, 8), 8)


def forward_x(pieces, q, tx, out):
    data = jnp.concatenate(
        [pieces[:, chunk_rows(q, h), :].reshape(2 * N, N) for h in range(GQ)], axis=1
    )
    high, low = split(data)
    tables = tx[...]
    both = mm(tables, high)
    tile = both[: 2 * M] + both[2 * M :] + mm(tables[: 2 * M], low)
    for h in range(GQ):
        for d in range(DP):
            for r in range(2):
                out[d, q * GQ + h, r] = tile[
                    r * M + 8 * d : r * M + 8 * d + 8, h * N : (h + 1) * N
                ]


def inverse_x(modes, q, ix, pieces):
    rows = jnp.concatenate(
        [
            jnp.concatenate([modes[:, q * GQ + h, r].reshape(M, N) for r in range(2)], axis=0)
            for h in range(GQ)
        ],
        axis=1,
    )
    high, low = split(rows)
    tile = mm(ix[...], jnp.concatenate([high, low, high], axis=0))
    for h in range(GQ):
        pieces[:, chunk_rows(q, h), :] = tile[:, h * N : (h + 1) * N].reshape(MP, 8, N)


def channel_matrix(matrix, expand, mat):
    spread_cols = lax.dot_general(
        matrix, expand, (((1,), (1,)), ((), ())), precision=lax.Precision.HIGHEST
    )
    full = jnp.dot(expand, spread_cols, precision=lax.Precision.HIGHEST)
    row = lax.broadcasted_iota(jnp.int32, (8 * C, 8 * C), 0)
    col = lax.broadcasted_iota(jnp.int32, (8 * C, 8 * C), 1)
    high, low = split(jnp.where(row % 8 == col % 8, full, 0.0))
    mat[: 8 * C] = high
    mat[8 * C :] = low


YB = 8


def channel_map(in_ref, x, mat, out_ref):
    @pl.loop(0, N // (8 * YB))
    def _(t):
        y = pl.multiple_of(t * 8 * YB, 8)
        data = jnp.concatenate(
            [in_ref[:, x, pl.ds(y + 8 * h, 8), :].reshape(8 * C, N) for h in range(YB)], axis=1
        )
        high, low = split(data)
        tables = mat[...]
        both = mm(tables, high)
        mapped = both[: 8 * C] + both[8 * C :] + mm(tables[: 8 * C], low)
        for h in range(YB):
            out_ref[:, x, pl.ds(y + 8 * h, 8), :] = mapped[:, h * N : (h + 1) * N].reshape(C, 8, N)


def factor_lanes():
    lane = lax.broadcasted_iota(jnp.int32, (8, N), 1)
    return jnp.where(lane % M == 0, 1.0, 2.0).astype(F32) * (1.0 / float(N * N * N))


def mix(spec_ref, w_ref, q, gather, sums, out_ref):
    @pl.loop(0, GQ)
    def _(h):
        for c in range(4):
            o = 4 * (q * GQ + h) + c
            acc = [[None, None] for _ in range(DP)]
            for i in range(CG):
                wr, wi = w_ref[0, i, o], w_ref[1, i, o]
                for b in range(DP):
                    sr, si = spec_ref[b, i, 0], spec_ref[b, i, 1]
                    re = wr * sr - wi * si
                    im = wr * si + wi * sr
                    acc[b] = [re, im] if i == 0 else [acc[b][0] + re, acc[b][1] + im]
            for b in range(DP):
                for r in range(2):
                    at = pl.ds(pl.multiple_of(h * 64 + (2 * b + r) * 8, 8), 8)
                    sums[at, c * N : (c + 1) * N] = acc[b][r]

    mixed = move_lanes(sums[...], gather)
    factor = factor_lanes()
    for h in range(GQ):
        for b in range(DP):
            for r in range(2):
                at = h * 64 + (2 * b + r) * 8
                out_ref[b, q * GQ + h, r] = mixed[at : at + 8] * factor


def spread(grad_ref, copy, rep_ref):
    factor = factor_lanes()
    rows = (grad_ref[...] * factor).reshape(DP * CG * 16, N)
    tiles = move_lanes(rows, copy)
    for b in range(DP):
        for g in range(CG):
            for r in range(2):
                at = ((b * CG + g) * 2 + r) * 8
                for c in range(4):
                    rep_ref[4 * g + c, b, r] = tiles[at : at + 8, c * N : (c + 1) * N]


def back_mix(rep_ref, w_ref, i, out_ref):
    def step(t, acc):
        acc = list(acc)
        for u in range(4):
            o = 4 * t + u
            wr, wi = w_ref[0, i, o], w_ref[1, i, o]
            for b in range(DP):
                gr, gi = rep_ref[o, b, 0], rep_ref[o, b, 1]
                acc[2 * b] = acc[2 * b] + (wr * gr + wi * gi)
                acc[2 * b + 1] = acc[2 * b + 1] + (wr * gi - wi * gr)
        return tuple(acc)

    acc = lax.fori_loop(0, 8, step, tuple(jnp.zeros((8, N), F32) for _ in range(8)))
    for b in range(DP):
        for r in range(2):
            out_ref[b, i, r] = acc[2 * b + r]


def weight_grad(rep_ref, spec_ref, o, out_ref):
    grads = [[rep_ref[o, b, r] for r in range(2)] for b in range(DP)]
    for i in range(CG):
        re = im = None
        for b in range(DP):
            gr, gi = grads[b]
            sr, si = spec_ref[b, i, 0], spec_ref[b, i, 1]
            r1 = gr * sr + gi * si
            i1 = gi * sr - gr * si
            re, im = (r1, i1) if b == 0 else (re + r1, im + i1)
        out_ref[0, i, o] = re
        out_ref[1, i, o] = im


def params(collective_id=None):
    if collective_id is None:
        return pltpu.CompilerParams(vmem_limit_bytes=VMEM_LIMIT)
    return pltpu.CompilerParams(
        vmem_limit_bytes=VMEM_LIMIT, collective_id=collective_id, has_side_effects=True
    )


def in_vmem():
    return pl.BlockSpec(memory_space=pltpu.VMEM)


def anywhere():
    return pl.BlockSpec(memory_space=pl.ANY)


def sems(count):
    return pltpu.SemaphoreType.DMA((count,))


SPEC = (DP, CG, 2, 8, N)
FLAT = (M * 64, N)
PIECES = (MP, 64, N)
CELLS = (C, XL, N, N)
PACKED = (2, CG, C, 8, N)


def to_spectrum(flat, pieces, held, out, tx, mp_sems, dp_sems):
    _, mp = position()

    def body(q):
        drain_mp(q, flat, mp_sems[1])
        pieces[mp, piece_rows(q)] = flat[flat_rows(mp, q)]
        forward_x(pieces, q, tx, held)
        send_dp(q, held, out, *dp_sems)
        keep_dp(q, held, out)

    chunks(body)


def move(q, modes, pieces, flat, ix, mp_sems, dp_recv):
    drain_dp(q, modes, dp_recv)
    inverse_x(modes, q, ix, pieces)
    send_to_cells(q, pieces, flat, *mp_sems)


def exchange_mixed(mix_chunk, mixed, modes, dp_sems):
    def body(q):
        mix_chunk(q)
        send_dp(q, mixed, modes, *dp_sems)
        keep_dp(q, mixed, modes)

    chunks(body)


STAGED = 3


def chunk_copy(src, dst, sem, q):
    part = pl.ds(q * 4 * GQ, 4 * GQ)
    return pltpu.make_async_copy(src.at[part], dst.at[part], sem.at[q])


def group_copy(src, dst, sem, g):
    part = pl.ds(4 * g, 4)
    return pltpu.make_async_copy(src.at[part], dst.at[part], sem.at[g])


def add_spectral(flat, g, iy, iz, cells):
    spectral = inverse_group(flat, g, iy, iz)
    for c in range(4):
        cells[4 * g + c] = cells[4 * g + c] + spectral[:, c * N : (c + 1) * N].reshape(XL, N, N)


def layer_kernel(
    field_ref, w_ref, up_ref, pw_ref, bias_ref, ex_ref,
    tz, ty, tx, ix, iy, iz, pack, gather, copy,
    flat_out, wgrad_out, point_out,
    fields, weight, upstream, cells, packed, rep, mat, sums,
    flat1, pieces1, held1, spectrum, mixed2, modes2, pieces2, flat2,
    flat3, pieces3, held3, grad_spec, mixed4, modes4, pieces4, flat4,
    field_sem, weight_sem, up_sem, point_sem,
    m1_send, m1_recv, d1_send, d1_recv, d2_send, d2_recv, m2_send, m2_recv,
    m3_send, m3_recv, d3_send, d3_recv, d4_send, d4_recv, m4_send, m4_recv,
):
    _, mp = position()
    greet()

    @pl.loop(0, STAGED)
    def _(g):
        group_copy(field_ref, fields, field_sem, g).start()

    def weight_copy(g):
        part = pl.ds(4 * g, 4)
        return pltpu.make_async_copy(w_ref.at[:, part], weight.at[:, part], weight_sem.at[g])

    def transform(g):
        weight_copy(g).start()
        group_copy(field_ref, fields, field_sem, g).wait()

        @pl.when(g < CG - STAGED)
        def _():
            group_copy(field_ref, fields, field_sem, g + STAGED).start()

        forward_group(fields, g, tz, ty, flat1)

    def field_chunk(q):
        groups_of(q, transform)

        @pl.when(q == 0)
        def _():
            await_greetings()

        send_to_modes(q, flat1, pieces1, m1_send, m1_recv)

    chunks(field_chunk)
    up_copy = pltpu.make_async_copy(up_ref, upstream, up_sem.at[0])
    up_copy.start()
    channel_matrix(pw_ref[...].T, ex_ref[...], mat)
    @pl.loop(0, CG)
    def _(g):
        weight_copy(g).wait()
        for r in range(2):
            tiles = [
                jnp.pad(weight[r, 4 * g + c].reshape(8 * C, M), ((0, 0), (0, N - M)))
                for c in range(4)
            ]
            packed[r, g] = move_lanes(jnp.concatenate(tiles, axis=1), pack).reshape(C, 8, N)

    to_spectrum(flat1, pieces1, held1, spectrum, tx, (m1_send, m1_recv), (d1_send, d1_recv))
    chunks(lambda q: drain_dp(q, spectrum, d1_recv))

    exchange_mixed(
        lambda q: mix(spectrum, packed, q, gather, sums, mixed2), mixed2, modes2, (d2_send, d2_recv)
    )

    def move_on(q):
        move(q, modes2, pieces2, flat2, ix, (m2_send, m2_recv), d2_recv)

    @pl.loop(0, AHEAD)
    def _(q):
        move_on(q)

    @pl.loop(0, XL)
    def _(x):
        channel_map(fields, x, mat, cells)

    up_copy.wait()

    def cell_group(g):
        spectral = inverse_group(flat2, g, iy, iz)
        for c in range(4):
            cells[4 * g + c] = (
                cells[4 * g + c]
                + spectral[:, c * N : (c + 1) * N].reshape(XL, N, N)
                + bias_ref[4 * g + c]
            )

        @pl.loop(0, 4 * XL)
        def _(t):
            o, x = 4 * g + t // XL, t % XL
            pre = cells[o, x]
            cdf = 0.5 * (1.0 + lax.erf(pre * np.float32(np.sqrt(0.5))))
            density = jnp.exp(-0.5 * pre * pre) * np.float32(1 / np.sqrt(2 * np.pi))
            cells[o, x] = upstream[o, x].astype(F32) * (cdf + pre * density)

        forward_group(cells, g, tz, ty, flat3)

    def cell_chunk(q):
        drain_mp(q, flat2, m2_recv)
        flat2[flat_rows(mp, q)] = pieces2[mp, piece_rows(q)]

        @pl.loop(0, GQ)
        def _(h):
            cell_group(q * GQ + h)

            @pl.when((h == 0) & (q < NQ - AHEAD))
            def _():
                move_on(q + AHEAD)

        send_to_modes(q, flat3, pieces3, m3_send, m3_recv)

    chunks(cell_chunk)
    channel_matrix(pw_ref[...], ex_ref[...], mat)
    to_spectrum(flat3, pieces3, held3, grad_spec, tx, (m3_send, m3_recv), (d3_send, d3_recv))
    chunks(lambda q: drain_dp(q, grad_spec, d3_recv))

    spread(grad_spec, copy, rep)
    exchange_mixed(
        lambda q: groups_of(q, lambda i: back_mix(rep, packed, i, mixed4)),
        mixed4, modes4, (d4_send, d4_recv),
    )

    @pl.loop(0, C)
    def _(o):
        weight_grad(rep, spectrum, o, wgrad_out)

    def move_back(q):
        move(q, modes4, pieces4, flat4, ix, (m4_send, m4_recv), d4_recv)

    chunks(move_back)

    @pl.loop(0, XL)
    def _(x):
        channel_map(cells, x, mat, fields)

    def land(q):
        drain_mp(q, flat4, m4_recv)
        flat4[flat_rows(mp, q)] = pieces4[mp, piece_rows(q)]

        @pl.when(q < NQ - LEFT)
        def _():
            groups_of(q, lambda g: add_spectral(flat4, g, iy, iz, fields))

        chunk_copy(fields, point_out, point_sem, q).start()

    chunks(land)
    flat_out[...] = flat4[...]
    for sem in (d1_send, d2_send, d3_send, d4_send):
        chunks(lambda q, sem=sem: drain_dp(q, mixed4, sem))

    for first, sem in ((0, m1_send), (0, m2_send), (0, m3_send), (0, m4_send)):

        @pl.loop(first, NQ)
        def _(q, sem=sem):
            drain_mp(q, flat4, sem)

    chunks(lambda q: chunk_copy(fields, point_out, point_sem, q).wait())


def layer(fields, weight, upstream, point_weight, point_bias):
    tabs = [TZ, TY, TX, IX, IY, IZ, PACK, GATHER, COPY]
    return pl.pallas_call(
        layer_kernel,
        in_specs=[anywhere(), anywhere(), anywhere(), in_vmem()]
        + [pl.BlockSpec(memory_space=pltpu.SMEM)]
        + [in_vmem()] * (1 + len(tabs)),
        out_specs=[in_vmem(), in_vmem(), anywhere()],
        out_shape=[
            jax.ShapeDtypeStruct(FLAT, F32),
            jax.ShapeDtypeStruct(PACKED, F32),
            jax.ShapeDtypeStruct(CELLS, F32),
        ],
        scratch_shapes=[
            pltpu.VMEM(CELLS, F32),
            pltpu.VMEM((2, C, C, 8, M), F32),
            pltpu.VMEM(CELLS, BF16),
            pltpu.VMEM(CELLS, F32),
            pltpu.VMEM(PACKED, F32),
            pltpu.VMEM((C, DP, 2, 8, N), F32),
            pltpu.VMEM((16 * C, 8 * C), BF16),
            pltpu.VMEM((GQ * 64, 4 * N), F32),
        ]
        + 2
        * [
            pltpu.VMEM(FLAT, F32),
            pltpu.VMEM(PIECES, F32),
            pltpu.VMEM(SPEC, F32),
            pltpu.VMEM(SPEC, F32),
            pltpu.VMEM(SPEC, F32),
            pltpu.VMEM(SPEC, F32),
            pltpu.VMEM(PIECES, F32),
            pltpu.VMEM(FLAT, F32),
        ]
        + [sems(CG), sems(CG), sems(1), sems(NQ)]
        + [sems(NQ)] * 16,
        compiler_params=params(1),
    )(
        fields,
        weight,
        upstream,
        point_weight,
        point_bias,
        jnp.asarray(EXPAND),
        *map(jnp.asarray, tabs),
    )


def finish_kernel(flat, point, wgrad, iy, iz, unpack, cells_out, wgrad_out):
    g = pl.program_id(0)

    @pl.when(g < CG - LEFT * GQ)
    def _():
        cells_out[...] = point[...]

    @pl.when(g >= CG - LEFT * GQ)
    def _():
        spectral = inverse_group(flat, g, iy, iz)
        for c in range(4):
            cells_out[c] = point[c] + spectral[:, c * N : (c + 1) * N].reshape(XL, N, N)

    tiles = move_lanes(wgrad[...].reshape(16 * C, N), unpack)
    for r in range(2):
        for c in range(4):
            wgrad_out[r, c] = tiles[
                r * 8 * C : (r + 1) * 8 * C, c * N : c * N + M
            ].reshape(C, 8, M)


def finish(flat, point, wgrad):
    cell_spec = pl.BlockSpec((4, XL, N, N), lambda g: (g, 0, 0, 0))
    return pl.pallas_call(
        finish_kernel,
        grid=(CG,),
        in_specs=[
            whole(FLAT),
            cell_spec,
            pl.BlockSpec((2, pl.Squeezed(), C, 8, N), lambda g: (0, g, 0, 0, 0)),
            whole(IY.shape),
            whole(IZ.shape),
            whole(UNPACK.shape),
        ],
        out_specs=[cell_spec, pl.BlockSpec((2, 4, C, 8, M), lambda g: (0, g, 0, 0, 0))],
        out_shape=[
            jax.ShapeDtypeStruct(CELLS, F32),
            jax.ShapeDtypeStruct((2, C, C, 8, M), F32),
        ],
        compiler_params=params(),
    )(flat, point, wgrad, *map(jnp.asarray, [IY, IZ, UNPACK]))


def shards(fields, upstream, spectral_weight, point_weight, point_bias):
    flat, wgrad, point = layer(
        fields[0], spectral_weight, upstream[0], point_weight, point_bias
    )
    grad_fields, weight_out = finish(flat, point, wgrad)
    return (grad_fields[None], weight_out)


def solution(mesh):
    placed = (
        P("dp", None, "mp", None, None),
        P("dp", None, "mp", None, None),
        P(None, None, None, "dp", "mp"),
        P(),
        P(),
    )
    return jax.shard_map(
        shards,
        mesh=mesh,
        in_specs=placed,
        out_specs=(P("dp", None, "mp", None, None), P(None, None, None, "dp", "mp")),
        check_vma=False,
    )
```
